256 devices in a mesh: prow: 8 (over z_lo, y), pcol: 32 (over z_hi, x, core).
Axes of the slice: x: 4, y: 4, z: 8 (z_hi: 4, z_lo: 2; z = z_hi * 2 + z_lo), core: 2. Of those that a mesh axis runs over, the one named last changes fastest.
Arguments:
- ancestor_inverse: bfloat16 [24576, 24576], P('prow', 'pcol'), may hold values from -6 to 6
- tile_pattern: int32 [64, 64], replicated, may hold values 0 or 1
- rows_first: int32 [24576], replicated, may hold values 0 or 1
- rows_second: int32 [24576], replicated, may hold values 0 or 1
- panel_first: bfloat16 [24576, 512], P('prow', 'pcol'), may hold values from -0.0390625 to 0.0390625
- panel_second: bfloat16 [24576, 512], P('prow', 'pcol'), may hold values from -0.21875 to 0.21875
- inner_panel: bfloat16 [512, 512], replicated, may hold values from -0.25 to 0.25
- pivot_first: float32 [512, 512], replicated, may hold values from -6 to 6
- pivot_second: float32 [512, 512], replicated, may hold values from -6 to 6
Outputs:
- column_first: bfloat16 [24576, 512], P(('prow', 'pcol'))
- diagonal_first: float32 [512, 512], replicated
- inner_second: float32 [512, 512], replicated
- column_second: bfloat16 [24576, 512], P(('prow', 'pcol'))
- diagonal_second: float32 [512, 512], replicated
The draws below stay inside these ranges and needn't reach their ends.
Inputs may be any that keep to these rules, and one draw needn't show every extreme that they name: `tile_pattern`: 1 marks a structurally nonzero tile. `rows_first`: 1 marks a row of the first supernode's structure. By construction here, a row belongs to the second supernode's structure only where both rows_second and rows_first are 1.
All inputs are finite; a program needn't handle non-finite values.
Results may differ from the reference program's by a relative error of at most 0.015.
Values may be sent and summed in bfloat16 or wider, within the bound.
A program may use at most 128 MiB of HBM per device.

```python
import jax
import jax.numpy as jnp
from jax import lax

R = 24576
W = 512
TILE = 384
NT = 64
N_PCOL = 32


def touch_ends(array, stream_key, least, largest):
    spot = [jax.random.randint(jax.random.fold_in(stream_key, axis), (), 0, length) for axis, length in enumerate(array.shape)]
    widest = array.shape.index(max(array.shape))
    beside = spot[:widest] + [(spot[widest] + 1) % array.shape[widest]] + spot[widest + 1:]
    return array.at[tuple(spot)].set(least).at[tuple(beside)].set(largest)


def spiked(values, stream_key, source, target, shards_of, factor):
    owner, partner = [(jnp.arange(values.shape[dim]) // (values.shape[dim] // shards_of)).reshape([-1 if axis == dim else 1 for axis in range(values.ndim)]) for dim in (source, target)]
    chosen = jax.random.permutation(stream_key, shards_of)[partner]
    strong = (owner == chosen) | (owner == (partner + shards_of // 2) % shards_of)
    return jnp.where(strong, factor * values, values)


def block_scale(key, dims, pieces, least, high):
    gain = 1.0
    for position, parts in pieces:
        draws = jax.random.uniform(jax.random.fold_in(jax.random.fold_in(key, 6), position), (parts,), jnp.float32, least / len(pieces), high / len(pieces))
        gain = gain * jnp.repeat(jnp.exp(draws), dims[position] // parts).reshape((-1,) + (1,) * (len(dims) - 1 - position))
    return gain


def gaussian(rng, extent, deviation, reach, cuts=(), kind=jnp.bfloat16):
    entries = deviation * jax.random.normal(rng, extent, jnp.float32)
    if cuts:
        entries = entries * block_scale(rng, extent, cuts, -0.22, 0.18)
    return jnp.clip(entries, -reach, reach).astype(kind)


def heavy_noise(key, extent, deviation, reach, cuts, heavy, kind=jnp.bfloat16):
    result = deviation * jax.random.normal(key, extent, jnp.float32)
    if cuts:
        result = result * block_scale(key, extent, cuts, -0.22, 0.18)
    return jnp.clip(spiked(result, jax.random.fold_in(key, 3), *heavy), -reach, reach).astype(kind)


def setup_inputs(seed: int = 0) -> dict:
    arg_keys = jax.random.split(jax.random.key(seed), 10)
    return {
        "ancestor_inverse": heavy_noise(arg_keys[0], (R, R), 1.0, 6.0, ((0, 8), (1, 32)), (1, 0, 32, 2.75)),
        "tile_pattern": touch_ends((jax.random.randint(arg_keys[1], (NT, NT), 0, 4) < 3).astype(jnp.int32), jax.random.fold_in(arg_keys[1], 1), 0, 1),
        "rows_first": touch_ends((jax.random.randint(arg_keys[2], (R,), 0, 2) < 1).astype(jnp.int32), jax.random.fold_in(arg_keys[2], 1), 0, 1),
        "rows_second": touch_ends((jax.random.randint(arg_keys[3], (R,), 0, 8) < 7).astype(jnp.int32), jax.random.fold_in(arg_keys[3], 1), 0, 1),
        "panel_first": gaussian(arg_keys[4], (R, W), R ** -0.5, 0.0390625, ((0, 8), (1, 32))),
        "panel_second": heavy_noise(arg_keys[5], (R, W), (R // 8) ** -0.5, 0.21875, ((0, 8), (1, 32)), (0, 1, 32, 2.75)),
        "inner_panel": gaussian(arg_keys[6], (W, W), W ** -0.5, 0.25),
        "pivot_first": gaussian(arg_keys[7], (W, W), 1.0, 6.0, (), jnp.float32),
        "pivot_second": gaussian(arg_keys[8], (W, W), 1.0, 6.0, (), jnp.float32),
    }


def mask_tiles(block, pattern, row_start, col_start):
    tile_rows = block.shape[0] // TILE
    tile_cols = block.shape[1] // TILE
    window = lax.dynamic_slice(pattern, (row_start, col_start), (tile_rows, tile_cols)).astype(jnp.bfloat16)
    shaped = block.reshape(tile_rows, TILE, tile_cols, TILE) * window[:, None, :, None]
    return shaped.reshape(block.shape)


def reference(ancestor_inverse, tile_pattern, rows_first, rows_second, panel_first, panel_second, inner_panel, pivot_first, pivot_second):
    struct_first = rows_first.astype(jnp.bfloat16)[:, None]
    struct_second = struct_first * rows_second.astype(jnp.bfloat16)[:, None]
    masked_first = panel_first * struct_first
    masked_second = panel_second * struct_second
    col_block = R // N_PCOL

    def step(carry, index):
        start = (index * col_block).astype(jnp.int32)
        block = lax.dynamic_slice_in_dim(ancestor_inverse, start, col_block, 1)
        block = mask_tiles(block, tile_pattern, jnp.int32(0), (index * (col_block // TILE)).astype(jnp.int32))
        first = lax.dynamic_slice_in_dim(masked_first, start, col_block, 0)
        second = lax.dynamic_slice_in_dim(masked_second, start, col_block, 0)
        term_first = lax.optimization_barrier(jnp.dot(block, first, preferred_element_type=jnp.float32).astype(jnp.bfloat16))
        term_second = lax.optimization_barrier(jnp.dot(block, second, preferred_element_type=jnp.float32).astype(jnp.bfloat16))
        return (carry[0] + term_first.astype(jnp.float32), carry[1] + term_second.astype(jnp.float32)), None

    zeros = jnp.zeros((R, W), jnp.float32)
    (sum_first, sum_second), _ = lax.scan(step, (zeros, zeros), jnp.arange(N_PCOL, dtype=jnp.int32))
    column_first = (-sum_first).astype(jnp.bfloat16)
    diagonal_first = pivot_first - jnp.dot(masked_first.T, column_first, preferred_element_type=jnp.float32)
    column_second = (-(sum_second + jnp.dot(column_first, inner_panel, preferred_element_type=jnp.float32))).astype(jnp.bfloat16)
    inner_wide = inner_panel.astype(jnp.float32)
    crossed = jnp.dot(column_first.T, masked_second, preferred_element_type=jnp.float32)
    inner_second = -(jnp.dot(diagonal_first, inner_wide, precision=lax.Precision.HIGHEST) + crossed)
    diagonal_second = pivot_second - jnp.dot(inner_wide.T, inner_second, precision=lax.Precision.HIGHEST) - jnp.dot(masked_second.T, column_second, preferred_element_type=jnp.float32)
    return column_first, diagonal_first, inner_second, column_second, diagonal_second
```

```python
import jax
import jax.numpy as jnp
from jax import lax
from jax.experimental import pallas as pl
from jax.experimental.pallas import tpu as pltpu
from jax.sharding import PartitionSpec as P

TILE = 384
MESH = pl.DeviceIdType.MESH
BF16 = jnp.bfloat16
F32 = jnp.float32

NY, NX, NZH, NZL, NC = 4, 4, 4, 2, 2
BLOCK = 768
SHARE = 96
W = 512


def nt_dot(left, right):
    return lax.dot_general(left, right, (((1,), (1,)), ((), ())), preferred_element_type=F32)


def nn_dot(left, right):
    return jnp.dot(left, right, preferred_element_type=F32)


class Links:
    def __init__(self, send_sem, recv_sem):
        self.send_sem = send_sem
        self.recv_sem = recv_sem
        self.used = 0
        self.pending = []

    def slot(self):
        self.used += 1
        return self.used - 1

    def make(self, src, dst, device, slot):
        return pltpu.make_async_remote_copy(
            src_ref=src,
            dst_ref=dst,
            send_sem=self.send_sem.at[slot],
            recv_sem=self.recv_sem.at[slot],
            device_id=device,
            device_id_type=MESH,
        )

    def send(self, src, dst, device, slot=None, unless=None):
        slot = self.slot() if slot is None else slot
        copy = self.make(src, dst, device, slot)
        if unless is None:
            copy.start()
        else:
            pl.when(jnp.logical_not(unless))(copy.start)
        self.pending.append((copy, unless))
        return slot

    def arrived(self, ref, device, slot, unless=None):
        copy = self.make(ref, ref, device, slot)
        if unless is None:
            copy.wait_recv()
        else:
            pl.when(jnp.logical_not(unless))(copy.wait_recv)

    def drain(self):
        for copy, unless in self.pending:
            if unless is None:
                copy.wait_send()
            else:
                pl.when(jnp.logical_not(unless))(copy.wait_send)
        self.pending = []


def kernel(
    a_ref,
    keep_ref,
    xt_ref,
    inner_ref,
    c1_ref,
    c2_ref,
    xg,
    ao,
    ax,
    pt,
    ptx,
    mx,
    t,
    town,
    rxd,
    rx,
    s1,
    s1own,
    rzd,
    rz,
    g,
    ys,
    yown,
    ry,
    zsrc,
    zrecv,
    zg,
    send_sem,
    recv_sem,
    local_sem,
):
    r = lax.axis_index("prow")
    c = lax.axis_index("pcol")
    y = r % NY
    zl = r // NY
    zh = c // 8
    x = (c // 2) % NX
    core = c % 2
    j = c % 8
    z = zh * 2 + zl

    def at(yy=None, zz=None, xx=None, cc=None):
        yy = y if yy is None else yy
        zz = z if zz is None else zz
        xx = x if xx is None else xx
        cc = core if cc is None else cc
        return ((zz % 2) * NY + yy, (zz // 2) * 8 + xx * 2 + cc)

    mate = at(cc=1 - core)
    xn, xp = at(xx=(x + 1) % NX), at(xx=(x + 3) % NX)
    zhn, zhp = at(zz=(z + 2) % 8), at(zz=(z + 6) % 8)
    yn, yp = at(yy=(y + 1) % NY), at(yy=(y + 3) % NY)
    zmate = at(zz=zh * 2 + 1 - zl)
    y_peers = [at(yy=(y + d) % NY) for d in range(1, NY)]
    z_peers = [at(zz=(z + d) % 8) for d in range(1, 8)]

    local_a = pltpu.make_async_copy(a_ref.at[:, :, core], ao, local_sem.at[0])
    local_a.start()

    barrier = pltpu.get_barrier_semaphore()
    first_self = c // 4 == r
    own_self = 8 * (c // 8) + c // 4 == c
    for device in [mate, xn, xp] + y_peers + z_peers:
        pl.semaphore_signal(barrier, inc=1, device_id=device, device_id_type=MESH)
    for i in range(4):

        @pl.when(jnp.logical_not(first_self & (c % 4 == i)))
        def _():
            pl.semaphore_signal(barrier, inc=1, device_id=(c // 4, 4 * r + i), device_id_type=MESH)

        @pl.when(jnp.logical_not(own_self & (c % 4 == i)))
        def _():
            pl.semaphore_signal(barrier, inc=1, device_id=(r, 4 * j + i), device_id_type=MESH)

    pl.semaphore_wait(
        barrier, 13 + 8 - first_self.astype(jnp.int32) - own_self.astype(jnp.int32)
    )

    links = Links(send_sem, recv_sem)

    slice16 = pl.ds(pl.multiple_of(16 * (c % 4), 16), 16)
    first_slots = [links.slot() for _ in range(4)]
    own_slots = [links.slot() for _ in range(4)]

    def piece(q):
        return xt_ref.at[:, :, pl.ds(768 * q, 768)]

    base_first, base_own = first_slots[0], own_slots[0]
    for q in range(4):
        me = first_self & (c % 4 == q)
        copy = pltpu.make_async_remote_copy(
            src_ref=piece(q),
            dst_ref=pt.at[c // 4, :, slice16, :],
            send_sem=send_sem.at[base_first + q],
            recv_sem=recv_sem.at[base_first + c % 4],
            device_id=(c // 4, 4 * r + q),
            device_id_type=MESH,
        )
        pl.when(jnp.logical_not(me))(copy.start)
        links.pending.append((copy, me))

        @pl.when(me)
        def _():
            local = pltpu.make_async_copy(piece(q), pt.at[c // 4, :, slice16, :], local_sem.at[1])
            local.start()
            local.wait()

    a_slot = links.send(a_ref.at[:, :, 1 - core], ax, mate)

    for q in range(4):
        me = own_self & (c // 8 == q)
        copy = pltpu.make_async_remote_copy(
            src_ref=piece(q),
            dst_ref=mx.at[:, slice16, :],
            send_sem=send_sem.at[base_own + q],
            recv_sem=recv_sem.at[base_own + c % 4],
            device_id=(r, 8 * q + c // 4),
            device_id_type=MESH,
        )
        pl.when(jnp.logical_not(me))(copy.start)
        links.pending.append((copy, me))

        @pl.when(me)
        def _():
            local = pltpu.make_async_copy(piece(q), mx.at[:, slice16, :], local_sem.at[2])
            local.start()
            local.wait()

    for i in range(4):
        links.arrived(
            pt.at[r, :, pl.ds(16 * i, 16), :],
            mate,
            base_first + i,
            first_self & (c % 4 == i),
        )

    def row_of(yy, zz):
        return zz * NY + yy

    r_z = row_of(y, 1 - zl)
    got_z = links.send(pt.at[r], pt.at[r], zmate)
    got_yp = links.send(pt.at[r], pt.at[r], yn)
    got_yn = links.send(pt.at[r], pt.at[r], yp)
    f_own = links.send(pt.at[r], ptx.at[r], mate)

    def mask_chunk(i, _):
        m = i // NX
        n = i % NX
        ao[m, n] = (ao[m, n].astype(F32) * keep_ref[0, m, n]).astype(BF16)
        return 0

    local_a.wait()
    lax.fori_loop(0, NZH * NX, mask_chunk, 0)

    links.arrived(pt.at[r_z], zmate, got_z)
    got_yp_z = links.send(pt.at[r_z], pt.at[r_z], yn)
    got_yn_z = links.send(pt.at[r_z], pt.at[r_z], yp)
    f_z = links.send(pt.at[r_z], ptx.at[r_z], mate)

    ry_p, ry_n, ry_d = (y + 3) % NY, (y + 1) % NY, (y + 2) % NY
    forwarded = [(r, f_own), (r_z, f_z)]
    relayed = []
    for zz, slot_p, slot_n in ((zl, got_yp, got_yn), (1 - zl, got_yp_z, got_yn_z)):
        row_p, row_n, row_d = row_of(ry_p, zz), row_of(ry_n, zz), row_of(ry_d, zz)
        links.arrived(pt.at[row_p], yp, slot_p)
        got_d0 = links.send(pt.at[row_p, 0], pt.at[row_p, 0], yn)
        links.arrived(pt.at[row_n], yn, slot_n)
        got_d1 = links.send(pt.at[row_n, 1], pt.at[row_n, 1], yp)
        forwarded.append((row_p, links.send(pt.at[row_p], ptx.at[row_p], mate)))
        forwarded.append((row_n, links.send(pt.at[row_n], ptx.at[row_n], mate)))
        relayed.append((row_d, got_d0, got_d1))
    links.arrived(ax, mate, a_slot)

    def mask_other(i, _):
        m = i // NX
        n = i % NX
        ax[m, n] = (ax[m, n].astype(F32) * keep_ref[1, m, n]).astype(BF16)
        return 0

    lax.fori_loop(0, NZH * NX, mask_other, 0)
    for row_d, got_d0, got_d1 in relayed:
        links.arrived(pt.at[row_d, 0], yp, got_d0)
        links.arrived(pt.at[row_d, 1], yn, got_d1)
        forwarded.append((row_d, links.send(pt.at[row_d], ptx.at[row_d], mate)))
    for row, slot in forwarded:
        links.arrived(ptx.at[row], mate, slot)

    def product(p, xx, out):
        left = ao[:, xx].reshape(NZH * SHARE, BLOCK)
        left_x = ax[:, xx].reshape(NZH * SHARE, BLOCK)
        for h in range(2):
            right = pt[pl.ds(4 * h, 4), p].reshape(256, BLOCK)
            right_x = ptx[pl.ds(4 * h, 4), p].reshape(256, BLOCK)
            value = nt_dot(left, right) + nt_dot(left_x, right_x)
            out[..., pl.ds(256 * h, 256)] = value.reshape(NZH, SHARE, 256).astype(out.dtype)

    slots = []
    for p in range(2):
        product(p, (x + 2) % NX, t.at[p, 0])
        got_p = links.send(t.at[p, 0, pl.ds(0, 2)], rxd.at[p, 0], xn)
        got_n = links.send(t.at[p, 0, pl.ds(2, 2)], rxd.at[p, 1], xp)
        product(p, (x + 1) % NX, t.at[p, 1])
        pure_p = links.send(t.at[p, 1, pl.ds(2, 2)], rx.at[p, 0, pl.ds(2, 2)], xn)
        product(p, (x + 3) % NX, t.at[p, 2])
        pure_n = links.send(t.at[p, 2, pl.ds(0, 2)], rx.at[p, 1, pl.ds(0, 2)], xp)
        product(p, x, town.at[p])
        slots.append((got_p, got_n, pure_p, pure_n))

    sums = []
    for p in range(2):
        got_p, got_n, pure_p, pure_n = slots[p]
        links.arrived(rxd.at[p, 0], xp, got_p)
        t[p, 1, 0:2] = (t[p, 1, 0:2].astype(F32) + rxd[p, 0].astype(F32)).astype(BF16)
        sum_p = links.send(t.at[p, 1, pl.ds(0, 2)], rx.at[p, 0, pl.ds(0, 2)], xn)
        links.arrived(rxd.at[p, 1], xn, got_n)
        t[p, 2, 2:4] = (t[p, 2, 2:4].astype(F32) + rxd[p, 1].astype(F32)).astype(BF16)
        sum_n = links.send(t.at[p, 2, pl.ds(2, 2)], rx.at[p, 1, pl.ds(2, 2)], xp)
        sums.append((sum_p, sum_n))

    half = SHARE // 2
    lo, hi = pl.ds(0, half), pl.ds(half, half)
    zh_n, zh_p, zh_d = (zh + 1) % NZH, (zh + 3) % NZH, (zh + 2) % NZH
    z_slots = []
    for p in range(2):
        _, _, pure_p, pure_n = slots[p]
        sum_p, sum_n = sums[p]
        links.arrived(rx.at[p, 0, pl.ds(2, 2)], xp, pure_p)
        links.arrived(rx.at[p, 1, pl.ds(0, 2)], xn, pure_n)
        links.arrived(rx.at[p, 0, pl.ds(0, 2)], xp, sum_p)
        links.arrived(rx.at[p, 1, pl.ds(2, 2)], xn, sum_n)

        def total(k):
            return town[p, k] + rx[p, 0, k].astype(F32) + rx[p, 1, k].astype(F32)

        s1[p, 0] = total(zh_d).astype(BF16)
        got_p = links.send(s1.at[p, 0, lo], rzd.at[p, 0], zhn)
        got_n = links.send(s1.at[p, 0, hi], rzd.at[p, 1], zhp)
        s1[p, 1] = total(zh_n).astype(BF16)
        pure_p = links.send(s1.at[p, 1, hi], rz.at[p, 0, hi], zhn)
        s1[p, 2] = total(zh_p).astype(BF16)
        pure_n = links.send(s1.at[p, 2, lo], rz.at[p, 1, lo], zhp)
        s1own[p] = total(zh)
        z_slots.append((got_p, got_n, pure_p, pure_n))

    z_sums = []
    for p in range(2):
        got_p, got_n, pure_p, pure_n = z_slots[p]
        links.arrived(rzd.at[p, 0], zhp, got_p)
        s1[p, 1, lo] = (s1[p, 1, lo].astype(F32) + rzd[p, 0].astype(F32)).astype(BF16)
        sum_p = links.send(s1.at[p, 1, lo], rz.at[p, 0, lo], zhn)
        links.arrived(rzd.at[p, 1], zhn, got_n)
        s1[p, 2, hi] = (s1[p, 2, hi].astype(F32) + rzd[p, 1].astype(F32)).astype(BF16)
        sum_n = links.send(s1.at[p, 2, hi], rz.at[p, 1, hi], zhp)
        z_sums.append((sum_p, sum_n))

    jn, jp, jd = (j + 2) % 8, (j + 6) % 8, (j + 4) % 8

    def gather_start(buf, fst, snd):
        own_p = links.send(buf(j), buf(j), xn)
        own_n = links.send(buf(j), buf(j), xp)
        own_m = links.send(buf(j), buf(j), mate)
        return own_p, own_n, own_m

    def gather_finish(buf, part, begun):
        own_p, own_n, own_m = begun
        links.arrived(buf(jp), xp, own_p)
        d0 = links.send(part(jp, 0), part(jp, 0), xn)
        links.arrived(buf(jn), xn, own_n)
        d1 = links.send(part(jn, 1), part(jn, 1), xp)
        m_p = links.send(buf(jp), buf(jp), mate)
        m_n = links.send(buf(jn), buf(jn), mate)
        links.arrived(part(jd, 0), xp, d0)
        links.arrived(part(jd, 1), xn, d1)
        m_d = links.send(buf(jd), buf(jd), mate)
        other = 1 - 2 * core
        links.arrived(buf(j + other), mate, own_m)
        links.arrived(buf(jp + other), mate, m_p)
        links.arrived(buf(jn + other), mate, m_n)
        links.arrived(buf(jd + other), mate, m_d)

    begun = []
    for p in range(2):
        _, _, pure_p, pure_n = z_slots[p]
        sum_p, sum_n = z_sums[p]
        links.arrived(rz.at[p, 0, hi], zhp, pure_p)
        links.arrived(rz.at[p, 1, lo], zhn, pure_n)
        links.arrived(rz.at[p, 0, lo], zhp, sum_p)
        links.arrived(rz.at[p, 1, hi], zhn, sum_n)
        total_sum = s1own[p] + rz[p, 0].astype(F32) + rz[p, 1].astype(F32)
        if p == 0:
            column = (-total_sum).astype(BF16)
            c1_ref[...] = column
        else:
            column = (-(total_sum + nn_dot(c1_ref[...], inner_ref[...]))).astype(BF16)
            c2_ref[...] = column
        g[p, j] = column
        begun.append(gather_start(lambda k: g.at[p, k], None, None))
    for p in range(2):
        gather_finish(
            lambda k: g.at[p, k],
            lambda k, h: g.at[p, k, pl.ds(half * h, half)],
            begun[p],
        )

    for i in range(4):
        links.arrived(
            mx.at[:, pl.ds(16 * i, 16), :],
            mate,
            base_own + i,
            own_self & (c % 4 == i),
        )
    for k, (m, p) in enumerate(((0, 0), (1, 0), (1, 1))):
        rows = nn_dot(mx[m], g[p].reshape(BLOCK, W))
        for d in range(NY):
            part = rows[:, 128 * d : 128 * d + 128]
            ys[d, pl.ds(64 * k, 64)] = part.astype(BF16)
            yown[d, pl.ds(64 * k, 64)] = part

    y_slots = []
    for d in range(1, NY):
        y_slots.append(links.send(ys.at[(y + d) % NY], ry.at[d - 1], y_peers[d - 1]))
    total_y = yown[y]
    for d in range(1, NY):
        links.arrived(ry.at[d - 1], y_peers[d - 1], y_slots[d - 1])
        total_y = total_y + ry[d - 1].astype(F32)
    zsrc[...] = total_y.reshape(8, 24, 128)
    z_rs = []
    for d in range(1, 8):
        z_rs.append(links.send(zsrc.at[(z + d) % 8], zrecv.at[d - 1], z_peers[d - 1]))
    total_z = zsrc[z]
    for d in range(1, 8):
        links.arrived(zrecv.at[d - 1], z_peers[d - 1], z_rs[d - 1])
        total_z = total_z + zrecv[d - 1]
    zg[z] = total_z
    z_ag = []
    for d in range(1, 8):
        z_ag.append(links.send(zg.at[z], zg.at[z], z_peers[d - 1]))
    for d in range(1, 8):
        links.arrived(zg.at[(z + 8 - d) % 8], z_peers[d - 1], z_ag[d - 1])
    xg[j, y] = zg[...].reshape(192, 128).astype(BF16)
    y_ag = []
    for d in range(1, NY):
        y_ag.append(links.send(xg.at[j, y], xg.at[j, y], y_peers[d - 1]))
    for d in range(1, NY):
        links.arrived(xg.at[j, (y + NY - d) % NY], y_peers[d - 1], y_ag[d - 1])
    begun_x = gather_start(lambda k: xg.at[k], None, None)
    gather_finish(
        lambda k: xg.at[k], lambda k, h: xg.at[k, pl.ds(2 * h, 2)], begun_x
    )
    links.drain()


N_COPIES = 128


def body(
    ancestor_inverse,
    tile_pattern,
    rows_first,
    rows_second,
    panel_first,
    panel_second,
    inner_panel,
    pivot_first,
    pivot_second,
):
    row_id = lax.axis_index("prow")
    col_id = lax.axis_index("pcol")
    row_block, col_block = ancestor_inverse.shape
    struct_first = lax.dynamic_slice_in_dim(rows_first, row_id * row_block, row_block).astype(BF16)
    struct_second = struct_first * lax.dynamic_slice_in_dim(
        rows_second, row_id * row_block, row_block
    ).astype(BF16)
    local = jnp.stack([panel_first.T * struct_first[None, :], panel_second.T * struct_second[None, :]])

    window = lax.dynamic_slice(
        tile_pattern, (row_id * (row_block // TILE), (col_id // 2) * 4), (row_block // TILE, 4)
    ).astype(F32)
    core = col_id % 2
    own = lax.dynamic_slice_in_dim(window, 2 * core, 2, 1)
    other = lax.dynamic_slice_in_dim(window, 2 * (1 - core), 2, 1)
    keep = jnp.stack([own, other])
    keep = keep.reshape(2, NZH, 2, 1, 1, 2, 1)
    keep = jnp.broadcast_to(keep, (2, NZH, 2, 2, 1, 2, TILE)).reshape(2, NZH, NX, 1, col_block)

    halves = ancestor_inverse.reshape(NZH, NX, NC, SHARE, col_block)
    anywhere = pl.BlockSpec(memory_space=pl.ANY)
    vmem = pl.BlockSpec(memory_space=pltpu.VMEM)
    column_first, column_second, gathered = pl.pallas_call(
        kernel,
        out_shape=(
            jax.ShapeDtypeStruct((SHARE, W), BF16),
            jax.ShapeDtypeStruct((SHARE, W), BF16),
            jax.ShapeDtypeStruct((8, NY, 192, 128), BF16),
        ),
        in_specs=[anywhere, vmem, vmem, vmem],
        out_specs=(vmem, vmem, vmem),
        scratch_shapes=[
            pltpu.VMEM((NZH, NX, SHARE, BLOCK), BF16),
            pltpu.VMEM((NZH, NX, SHARE, BLOCK), BF16),
            pltpu.VMEM((8, 2, 64, BLOCK), BF16),
            pltpu.VMEM((8, 2, 64, BLOCK), BF16),
            pltpu.VMEM((2, 64, BLOCK), BF16),
            pltpu.VMEM((2, 3, NZH, SHARE, W), BF16),
            pltpu.VMEM((2, NZH, SHARE, W), F32),
            pltpu.VMEM((2, 2, 2, SHARE, W), BF16),
            pltpu.VMEM((2, 2, NZH, SHARE, W), BF16),
            pltpu.VMEM((2, 3, SHARE, W), BF16),
            pltpu.VMEM((2, SHARE, W), F32),
            pltpu.VMEM((2, 2, SHARE // 2, W), BF16),
            pltpu.VMEM((2, 2, SHARE, W), BF16),
            pltpu.VMEM((2, 8, SHARE, W), BF16),
            pltpu.VMEM((NY, 192, 128), BF16),
            pltpu.VMEM((NY, 192, 128), F32),
            pltpu.VMEM((NY - 1, 192, 128), BF16),
            pltpu.VMEM((8, 24, 128), F32),
            pltpu.VMEM((7, 24, 128), F32),
            pltpu.VMEM((8, 24, 128), F32),
            pltpu.SemaphoreType.DMA((N_COPIES,)),
            pltpu.SemaphoreType.DMA((N_COPIES,)),
            pltpu.SemaphoreType.DMA((3,)),
        ],
        compiler_params=pltpu.CompilerParams(
            collective_id=0, has_side_effects=True, vmem_limit_bytes=48 * 2**20
        ),
    )(halves, keep, local, inner_panel)

    products = gathered.reshape(8, NY, 3, 64, 128).transpose(2, 0, 3, 1, 4).reshape(3, W, W).astype(F32)
    corr_first, crossed_t, corr_second = products[0], products[1], products[2]
    diagonal_first = pivot_first - corr_first
    inner_wide = inner_panel.astype(F32)
    inner_second = -(
        jnp.dot(diagonal_first, inner_wide, precision=lax.Precision.HIGHEST) + crossed_t.T
    )
    diagonal_second = (
        pivot_second
        - jnp.dot(inner_wide.T, inner_second, precision=lax.Precision.HIGHEST)
        - corr_second
    )
    return (column_first, diagonal_first, inner_second, column_second, diagonal_second)


def solution(mesh):
    return jax.shard_map(
        body,
        mesh=mesh,
        in_specs=(
            P("prow", "pcol"),
            P(),
            P(),
            P(),
            P("prow", "pcol"),
            P("prow", "pcol"),
            P(),
            P(),
            P(),
        ),
        out_specs=(P(("prow", "pcol"), None), P(), P(), P(("prow", "pcol"), None), P()),
        check_vma=False,
    )
```

```python
import jax
import jax.numpy as jnp
from jax import lax
from jax.experimental import pallas as pl
from jax.experimental.pallas import tpu as pltpu
from jax.sharding import PartitionSpec as P

TILE = 384
MESH = pl.DeviceIdType.MESH
BF16 = jnp.bfloat16
F32 = jnp.float32

NY, NX, NZH, NZL, NC = 4, 4, 4, 2, 2
BLOCK = 768
SHARE = 96
W = 512


def nt_dot(left, right):
    return lax.dot_general(left, right, (((1,), (1,)), ((), ())), preferred_element_type=F32)


def nn_dot(left, right):
    return jnp.dot(left, right, preferred_element_type=F32)


class Links:
    def __init__(self, send_sem, recv_sem):
        self.send_sem = send_sem
        self.recv_sem = recv_sem
        self.used = 0
        self.pending = []

    def slot(self):
        self.used += 1
        return self.used - 1

    def make(self, src, dst, device, slot):
        return pltpu.make_async_remote_copy(
            src_ref=src,
            dst_ref=dst,
            send_sem=self.send_sem.at[slot],
            recv_sem=self.recv_sem.at[slot],
            device_id=device,
            device_id_type=MESH,
        )

    def send(self, src, dst, device, slot=None, unless=None):
        slot = self.slot() if slot is None else slot
        copy = self.make(src, dst, device, slot)
        if unless is None:
            copy.start()
        else:
            pl.when(jnp.logical_not(unless))(copy.start)
        self.pending.append((copy, unless))
        return slot

    def arrived(self, ref, device, slot, unless=None):
        copy = self.make(ref, ref, device, slot)
        if unless is None:
            copy.wait_recv()
        else:
            pl.when(jnp.logical_not(unless))(copy.wait_recv)

    def drain(self):
        for copy, unless in self.pending:
            if unless is None:
                copy.wait_send()
            else:
                pl.when(jnp.logical_not(unless))(copy.wait_send)
        self.pending = []


def kernel(
    a_ref,
    pattern_ref,
    panel1_ref,
    panel2_ref,
    rows1_ref,
    rows2_ref,
    inner_ref,
    c1_ref,
    c2_ref,
    xg0,
    xg1,
    ao,
    ax,
    pattern,
    panels,
    rows,
    inner,
    xt,
    pt,
    ptx,
    mx,
    t,
    town,
    rxd,
    rx,
    s1,
    s1own,
    rzd,
    rz,
    g,
    ys,
    yown,
    ry,
    zsrc0,
    zrecv0,
    zg0,
    zsrc1,
    zrecv1,
    zg1,
    send_sem,
    recv_sem,
    local_sem,
):
    r = lax.axis_index("prow")
    c = lax.axis_index("pcol")
    y = r % NY
    zl = r // NY
    zh = c // 8
    x = (c // 2) % NX
    core = c % 2
    j = c % 8
    z = zh * 2 + zl

    def at(yy=None, zz=None, xx=None, cc=None):
        yy = y if yy is None else yy
        zz = z if zz is None else zz
        xx = x if xx is None else xx
        cc = core if cc is None else cc
        return ((zz % 2) * NY + yy, (zz // 2) * 8 + xx * 2 + cc)

    mate = at(cc=1 - core)
    xn, xp = at(xx=(x + 1) % NX), at(xx=(x + 3) % NX)
    zhn, zhp = at(zz=(z + 2) % 8), at(zz=(z + 6) % 8)
    yn, yp = at(yy=(y + 1) % NY), at(yy=(y + 3) % NY)
    zmate = at(zz=zh * 2 + 1 - zl)
    y_peers = [at(yy=(y + d) % NY) for d in range(1, NY)]
    z_peers = [at(zz=(z + d) % 8) for d in range(1, 8)]

    barrier = pltpu.get_barrier_semaphore()
    first_self = c // 4 == r
    own_self = 8 * (c // 8) + c // 4 == c
    for device in [mate, xn, xp] + y_peers + z_peers:
        pl.semaphore_signal(barrier, inc=1, device_id=device, device_id_type=MESH)
    for i in range(4):

        @pl.when(jnp.logical_not(first_self & (c % 4 == i)))
        def _():
            pl.semaphore_signal(barrier, inc=1, device_id=(c // 4, 4 * r + i), device_id_type=MESH)

        @pl.when(jnp.logical_not(own_self & (c % 4 == i)))
        def _():
            pl.semaphore_signal(barrier, inc=1, device_id=(r, 4 * j + i), device_id_type=MESH)

    own_rows = pl.ds(pl.multiple_of(24 * r, 8), 24)
    loads = [
        pltpu.make_async_copy(rows1_ref.at[own_rows], rows.at[0], local_sem.at[3]),
        pltpu.make_async_copy(rows2_ref.at[own_rows], rows.at[1], local_sem.at[4]),
        pltpu.make_async_copy(panel1_ref, panels.at[0], local_sem.at[5]),
        pltpu.make_async_copy(panel2_ref, panels.at[1], local_sem.at[6]),
        pltpu.make_async_copy(pattern_ref, pattern, local_sem.at[7]),
        pltpu.make_async_copy(a_ref.at[:, :, core], ao, local_sem.at[0]),
        pltpu.make_async_copy(inner_ref, inner, local_sem.at[8]),
    ]
    for load in loads:
        load.start()
    for load in loads[:4]:
        load.wait()
    keep1 = rows[0].astype(F32)
    keep2 = keep1 * rows[1].astype(F32)
    for p, keep in enumerate((keep1, keep2)):
        for k in range(24):
            cut = slice(128 * k, 128 * k + 128)
            xt[p, :, cut] = (panels[p, :, cut].astype(F32) * keep[k : k + 1]).astype(BF16)

    pl.semaphore_wait(
        barrier, 13 + 8 - first_self.astype(jnp.int32) - own_self.astype(jnp.int32)
    )

    links = Links(send_sem, recv_sem)

    slice16 = pl.ds(pl.multiple_of(16 * (c % 4), 16), 16)
    base_first = [links.slot() for _ in range(8)][0]
    base_own = [links.slot() for _ in range(4)][0]

    def spread(source, target, base, device, me, q, spare):
        copy = pltpu.make_async_remote_copy(
            src_ref=source,
            dst_ref=target,
            send_sem=send_sem.at[base + q],
            recv_sem=recv_sem.at[base + c % 4],
            device_id=device,
            device_id_type=MESH,
        )
        pl.when(jnp.logical_not(me))(copy.start)
        links.pending.append((copy, me))

        @pl.when(me)
        def _():
            local = pltpu.make_async_copy(source, target, local_sem.at[spare])
            local.start()
            local.wait()

    for p in range(2):
        for q in range(4):
            spread(
                xt.at[p, :, pl.ds(768 * q, 768)],
                pt.at[c // 4, p, slice16, :],
                base_first + 4 * p,
                (c // 4, 4 * r + q),
                first_self & (c % 4 == q),
                q,
                1,
            )

    a_slot = links.send(a_ref.at[:, :, 1 - core], ax, mate)

    for q in range(4):
        spread(
            xt.at[:, :, pl.ds(768 * q, 768)],
            mx.at[:, slice16, :],
            base_own,
            (r, 8 * q + c // 4),
            own_self & (c // 8 == q),
            q,
            2,
        )

    def mask_rows(ref, owner):
        def chunk(i, _):
            m = i // NX
            n = i % NX
            for k in range(2):
                cut = slice(TILE * k, TILE * k + TILE)
                keep = pattern[8 * r + 2 * m + n // 2, 2 * owner + k].astype(F32)
                ref[m, n, :, cut] = (ref[m, n, :, cut].astype(F32) * keep).astype(BF16)
            return 0

        lax.fori_loop(0, NZH * NX, chunk, 0)

    for load in loads[4:]:
        load.wait()
    mask_rows(ao, c)

    def row_of(yy, zz):
        return zz * NY + yy

    r_z = row_of(y, 1 - zl)
    y_p, y_n, y_d = (y + 3) % NY, (y + 1) % NY, (y + 2) % NY

    def panel_gather(p):
        forwarded = []

        def to(device, row):
            return links.send(pt.at[row, p], pt.at[row, p], device)

        def to_mate(row):
            forwarded.append((row, links.send(pt.at[row, p], ptx.at[row, p], mate)))

        def part(row, h):
            return pt.at[row, p, pl.ds(32 * h, 32)]

        for i in range(4):
            links.arrived(
                pt.at[r, p, pl.ds(16 * i, 16), :],
                mate,
                base_first + 4 * p + i,
                first_self & (c % 4 == i),
            )
        got_z, got_yp, got_yn = to(zmate, r), to(yn, r), to(yp, r)
        to_mate(r)
        yield
        links.arrived(pt.at[r_z, p], zmate, got_z)
        got_yp_z, got_yn_z = to(yn, r_z), to(yp, r_z)
        to_mate(r_z)
        yield
        relayed = []
        for zz, slot_p, slot_n in ((zl, got_yp, got_yn), (1 - zl, got_yp_z, got_yn_z)):
            row_p, row_n, row_d = row_of(y_p, zz), row_of(y_n, zz), row_of(y_d, zz)
            links.arrived(pt.at[row_p, p], yp, slot_p)
            got_d0 = links.send(part(row_p, 0), part(row_p, 0), yn)
            links.arrived(pt.at[row_n, p], yn, slot_n)
            got_d1 = links.send(part(row_n, 1), part(row_n, 1), yp)
            to_mate(row_p)
            to_mate(row_n)
            relayed.append((row_d, got_d0, got_d1))
            yield
        for row_d, got_d0, got_d1 in relayed:
            links.arrived(part(row_d, 0), yp, got_d0)
            links.arrived(part(row_d, 1), yn, got_d1)
            to_mate(row_d)
        yield
        for row, slot in forwarded:
            links.arrived(ptx.at[row, p], mate, slot)
        yield

    def product(p, xx, out):
        left = ao[:, xx].reshape(NZH * SHARE, BLOCK)
        left_x = ax[:, xx].reshape(NZH * SHARE, BLOCK)
        for h in range(2):
            right = pt[pl.ds(4 * h, 4), p].reshape(256, BLOCK)
            right_x = ptx[pl.ds(4 * h, 4), p].reshape(256, BLOCK)
            value = nt_dot(left, right) + nt_dot(left_x, right_x)
            out[..., pl.ds(256 * h, 256)] = value.reshape(NZH, SHARE, 256).astype(out.dtype)

    half = SHARE // 2
    lo, hi = pl.ds(0, half), pl.ds(half, half)
    zh_n, zh_p, zh_d = (zh + 1) % NZH, (zh + 3) % NZH, (zh + 2) % NZH
    jn, jp, jd = (j + 2) % 8, (j + 6) % 8, (j + 4) % 8

    def over_x_core(buf, part):
        own_p = links.send(buf(j), buf(j), xn)
        own_n = links.send(buf(j), buf(j), xp)
        own_m = links.send(buf(j), buf(j), mate)
        yield
        links.arrived(buf(jp), xp, own_p)
        d0 = links.send(part(jp, 0), part(jp, 0), xn)
        links.arrived(buf(jn), xn, own_n)
        d1 = links.send(part(jn, 1), part(jn, 1), xp)
        m_p = links.send(buf(jp), buf(jp), mate)
        m_n = links.send(buf(jn), buf(jn), mate)
        yield
        links.arrived(part(jd, 0), xp, d0)
        links.arrived(part(jd, 1), xn, d1)
        m_d = links.send(buf(jd), buf(jd), mate)
        yield
        other = 1 - 2 * core
        links.arrived(buf(j + other), mate, own_m)
        links.arrived(buf(jp + other), mate, m_p)
        links.arrived(buf(jn + other), mate, m_n)
        links.arrived(buf(jd + other), mate, m_d)

    def chain(p):
        product(p, (x + 2) % NX, t.at[p, 0])
        got_p = links.send(t.at[p, 0, pl.ds(0, 2)], rxd.at[p, 0], xn)
        got_n = links.send(t.at[p, 0, pl.ds(2, 2)], rxd.at[p, 1], xp)
        yield
        product(p, (x + 1) % NX, t.at[p, 1])
        pure_p = links.send(t.at[p, 1, pl.ds(2, 2)], rx.at[p, 0, pl.ds(2, 2)], xn)
        yield
        product(p, (x + 3) % NX, t.at[p, 2])
        pure_n = links.send(t.at[p, 2, pl.ds(0, 2)], rx.at[p, 1, pl.ds(0, 2)], xp)
        yield
        product(p, x, town.at[p])
        yield
        links.arrived(rxd.at[p, 0], xp, got_p)
        t[p, 1, 0:2] = (t[p, 1, 0:2].astype(F32) + rxd[p, 0].astype(F32)).astype(BF16)
        sum_p = links.send(t.at[p, 1, pl.ds(0, 2)], rx.at[p, 0, pl.ds(0, 2)], xn)
        links.arrived(rxd.at[p, 1], xn, got_n)
        t[p, 2, 2:4] = (t[p, 2, 2:4].astype(F32) + rxd[p, 1].astype(F32)).astype(BF16)
        sum_n = links.send(t.at[p, 2, pl.ds(2, 2)], rx.at[p, 1, pl.ds(2, 2)], xp)
        yield
        links.arrived(rx.at[p, 0, pl.ds(2, 2)], xp, pure_p)
        links.arrived(rx.at[p, 1, pl.ds(0, 2)], xn, pure_n)
        links.arrived(rx.at[p, 0, pl.ds(0, 2)], xp, sum_p)
        links.arrived(rx.at[p, 1, pl.ds(2, 2)], xn, sum_n)

        def total(k):
            return town[p, k] + rx[p, 0, k].astype(F32) + rx[p, 1, k].astype(F32)

        s1[p, 0] = total(zh_d).astype(BF16)
        got_p = links.send(s1.at[p, 0, lo], rzd.at[p, 0], zhn)
        got_n = links.send(s1.at[p, 0, hi], rzd.at[p, 1], zhp)
        s1[p, 1] = total(zh_n).astype(BF16)
        pure_p = links.send(s1.at[p, 1, hi], rz.at[p, 0, hi], zhn)
        s1[p, 2] = total(zh_p).astype(BF16)
        pure_n = links.send(s1.at[p, 2, lo], rz.at[p, 1, lo], zhp)
        s1own[p] = total(zh)
        yield
        links.arrived(rzd.at[p, 0], zhp, got_p)
        s1[p, 1, lo] = (s1[p, 1, lo].astype(F32) + rzd[p, 0].astype(F32)).astype(BF16)
        sum_p = links.send(s1.at[p, 1, lo], rz.at[p, 0, lo], zhn)
        links.arrived(rzd.at[p, 1], zhn, got_n)
        s1[p, 2, hi] = (s1[p, 2, hi].astype(F32) + rzd[p, 1].astype(F32)).astype(BF16)
        sum_n = links.send(s1.at[p, 2, hi], rz.at[p, 1, hi], zhp)
        yield
        links.arrived(rz.at[p, 0, hi], zhp, pure_p)
        links.arrived(rz.at[p, 1, lo], zhn, pure_n)
        links.arrived(rz.at[p, 0, lo], zhp, sum_p)
        links.arrived(rz.at[p, 1, hi], zhn, sum_n)
        total_sum = s1own[p] + rz[p, 0].astype(F32) + rz[p, 1].astype(F32)
        if p == 0:
            column = (-total_sum).astype(BF16)
            c1_ref[...] = column
        else:
            column = (-(total_sum + nn_dot(c1_ref[...], inner[...]))).astype(BF16)
            c2_ref[...] = column
        g[p, j] = column
        yield from over_x_core(
            lambda k: g.at[p, k], lambda k, h: g.at[p, k, pl.ds(half * h, half)]
        )

        if p == 0:
            for i in range(4):
                links.arrived(
                    mx.at[:, pl.ds(16 * i, 16), :],
                    mate,
                    base_own + i,
                    own_self & (c % 4 == i),
                )
        sides = (0, 1) if p == 0 else (1,)
        n = 64 * len(sides)
        xg, zsrc, zrecv, zg = ((xg0, zsrc0, zrecv0, zg0), (xg1, zsrc1, zrecv1, zg1))[p]
        for k, m in enumerate(sides):
            found = nn_dot(mx[m], g[p].reshape(BLOCK, W))
            for d in range(NY):
                part = found[:, 128 * d : 128 * d + 128]
                ys[p, d, pl.ds(64 * k, 64)] = part.astype(BF16)
                yown[p, d, pl.ds(64 * k, 64)] = part
        cut = pl.ds(0, n)
        y_rs = [
            links.send(ys.at[p, (y + d) % NY, cut], ry.at[p, d - 1, cut], y_peers[d - 1])
            for d in range(1, NY)
        ]
        yield
        total_y = yown[p, y, 0:n]
        for d in range(1, NY):
            links.arrived(ry.at[p, d - 1, cut], y_peers[d - 1], y_rs[d - 1])
            total_y = total_y + ry[p, d - 1, 0:n].astype(F32)
        zsrc[...] = total_y.reshape(8, n // 8, 128)
        z_rs = [
            links.send(zsrc.at[(z + d) % 8], zrecv.at[d - 1], z_peers[d - 1]) for d in range(1, 8)
        ]
        yield
        total_z = zsrc[z]
        for d in range(1, 8):
            links.arrived(zrecv.at[d - 1], z_peers[d - 1], z_rs[d - 1])
            total_z = total_z + zrecv[d - 1]
        zg[z] = total_z
        z_ag = [links.send(zg.at[z], zg.at[z], z_peers[d - 1]) for d in range(1, 8)]
        yield
        for d in range(1, 8):
            links.arrived(zg.at[(z + 8 - d) % 8], z_peers[d - 1], z_ag[d - 1])
        xg[j, y] = zg[...].reshape(n, 128).astype(BF16)
        y_ag = [links.send(xg.at[j, y], xg.at[j, y], y_peers[d - 1]) for d in range(1, NY)]
        yield
        for d in range(1, NY):
            links.arrived(xg.at[j, (y + NY - d) % NY], y_peers[d - 1], y_ag[d - 1])
        yield from over_x_core(lambda k: xg.at[k], lambda k, h: xg.at[k, pl.ds(2 * h, 2)])
        yield

    parts = {
        "f": panel_gather(0),
        "s": panel_gather(1),
        "A": chain(0),
        "B": chain(1),
    }
    for name in "ff" + "s" + "m" + "ff" + "s" + "f" + "s" + "f" + ORDER:
        if name == "m":
            links.arrived(ax, mate, a_slot)
            mask_rows(ax, c + 1 - 2 * core)
        else:
            next(parts[name])
    links.drain()


ORDER = "AsAsAAs" + "BABBBA" + "BAAABAABABABABABABABAB" + "BBBB"
N_COPIES = 160


def finish(
    inner_ref, pivot1_ref, pivot2_ref, xg0, xg1, d1_out, i2_out, d2_out, d1, i2, d2, crossed, sem
):
    def assemble(out, source, first, pivot):
        for k in range(8):
            for d in range(NY):
                rows, cols = slice(64 * k, 64 * k + 64), slice(128 * d, 128 * d + 128)
                part = source[k, d, first : first + 64].astype(F32)
                out[rows, cols] = part if pivot is None else pivot[rows, cols] - part

    def parts_dot(dot, wide):
        high = wide.astype(BF16)
        low = (wide - high.astype(F32)).astype(BF16)
        return dot(high) + dot(low)

    inner = inner_ref[...]
    assemble(d1, xg0, 0, pivot1_ref)
    copies = [pltpu.make_async_copy(d1, d1_out, sem.at[0])]
    copies[0].start()
    assemble(crossed, xg0, 64, None)
    i2[...] = -(parts_dot(lambda v: nn_dot(v, inner), d1[...]) + crossed[...].T)
    copies.append(pltpu.make_async_copy(i2, i2_out, sem.at[1]))
    copies[1].start()
    inner_t = inner.T
    assemble(d2, xg1, 0, pivot2_ref)
    d2[...] = d2[...] - parts_dot(lambda v: nn_dot(inner_t, v), i2[...])
    copies.append(pltpu.make_async_copy(d2, d2_out, sem.at[2]))
    copies[2].start()
    for copy in copies:
        copy.wait()


def body(
    ancestor_inverse,
    tile_pattern,
    rows_first,
    rows_second,
    panel_first,
    panel_second,
    inner_panel,
    pivot_first,
    pivot_second,
):
    col_block = ancestor_inverse.shape[1]
    halves = ancestor_inverse.reshape(NZH, NX, NC, SHARE, col_block)
    anywhere = pl.BlockSpec(memory_space=pl.ANY)
    vmem = pl.BlockSpec(memory_space=pltpu.VMEM)
    wide = jax.ShapeDtypeStruct((W, W), F32)
    column_first, column_second, gathered0, gathered1 = pl.pallas_call(
        kernel,
        out_shape=(
            jax.ShapeDtypeStruct((SHARE, W), BF16),
            jax.ShapeDtypeStruct((SHARE, W), BF16),
            jax.ShapeDtypeStruct((8, NY, 128, 128), BF16),
            jax.ShapeDtypeStruct((8, NY, 64, 128), BF16),
        ),
        in_specs=[anywhere] * 7,
        out_specs=(vmem, vmem, vmem, vmem),
        scratch_shapes=[
            pltpu.VMEM((NZH, NX, SHARE, BLOCK), BF16),
            pltpu.VMEM((NZH, NX, SHARE, BLOCK), BF16),
            pltpu.SMEM((64, 64), jnp.int32),
            pltpu.VMEM((2, 16, 3072), BF16),
            pltpu.VMEM((2, 24, 128), jnp.int32),
            pltpu.VMEM((W, W), BF16),
            pltpu.VMEM((2, 16, 3072), BF16),
            pltpu.VMEM((8, 2, 64, BLOCK), BF16),
            pltpu.VMEM((8, 2, 64, BLOCK), BF16),
            pltpu.VMEM((2, 64, BLOCK), BF16),
            pltpu.VMEM((2, 3, NZH, SHARE, W), BF16),
            pltpu.VMEM((2, NZH, SHARE, W), F32),
            pltpu.VMEM((2, 2, 2, SHARE, W), BF16),
            pltpu.VMEM((2, 2, NZH, SHARE, W), BF16),
            pltpu.VMEM((2, 3, SHARE, W), BF16),
            pltpu.VMEM((2, SHARE, W), F32),
            pltpu.VMEM((2, 2, SHARE // 2, W), BF16),
            pltpu.VMEM((2, 2, SHARE, W), BF16),
            pltpu.VMEM((2, 8, SHARE, W), BF16),
            pltpu.VMEM((2, NY, 128, 128), BF16),
            pltpu.VMEM((2, NY, 128, 128), F32),
            pltpu.VMEM((2, NY - 1, 128, 128), BF16),
            pltpu.VMEM((8, 16, 128), F32),
            pltpu.VMEM((7, 16, 128), F32),
            pltpu.VMEM((8, 16, 128), F32),
            pltpu.VMEM((8, 8, 128), F32),
            pltpu.VMEM((7, 8, 128), F32),
            pltpu.VMEM((8, 8, 128), F32),
            pltpu.SemaphoreType.DMA((N_COPIES,)),
            pltpu.SemaphoreType.DMA((N_COPIES,)),
            pltpu.SemaphoreType.DMA((9,)),
        ],
        compiler_params=pltpu.CompilerParams(
            collective_id=0, has_side_effects=True, vmem_limit_bytes=48 * 2**20
        ),
    )(
        halves,
        tile_pattern,
        panel_first.T,
        panel_second.T,
        rows_first.reshape(-1, 128),
        rows_second.reshape(-1, 128),
        inner_panel,
    )
    diagonal_first, inner_second, diagonal_second = pl.pallas_call(
        finish,
        out_shape=(wide, wide, wide),
        in_specs=[vmem] * 5,
        out_specs=(anywhere,) * 3,
        scratch_shapes=[pltpu.VMEM((W, W), F32)] * 4 + [pltpu.SemaphoreType.DMA((3,))],
        compiler_params=pltpu.CompilerParams(vmem_limit_bytes=32 * 2**20),
    )(inner_panel, pivot_first, pivot_second, gathered0, gathered1)
    return (column_first, diagonal_first, inner_second, column_second, diagonal_second)


def solution(mesh):
    return jax.shard_map(
        body,
        mesh=mesh,
        in_specs=(
            P("prow", "pcol"),
            P(),
            P(),
            P(),
            P("prow", "pcol"),
            P("prow", "pcol"),
            P(),
            P(),
            P(),
        ),
        out_specs=(P(("prow", "pcol"), None), P(), P(), P(("prow", "pcol"), None), P()),
        check_vma=False,
    )
```

```python
import jax
import jax.numpy as jnp
from jax import lax
from jax.experimental import pallas as pl
from jax.experimental.pallas import tpu as pltpu
from jax.sharding import PartitionSpec as P

TILE = 384
MESH = pl.DeviceIdType.MESH
BF16 = jnp.bfloat16
F32 = jnp.float32

NY, NX, NZH, NZL, NC = 4, 4, 4, 2, 2
BLOCK = 768
SHARE = 96
W = 512


def nt_dot(left, right):
    return lax.dot_general(left, right, (((1,), (1,)), ((), ())), preferred_element_type=F32)


def nn_dot(left, right):
    return jnp.dot(left, right, preferred_element_type=F32)


class Links:
    def __init__(self, send_sem, recv_sem):
        self.send_sem = send_sem
        self.recv_sem = recv_sem
        self.used = 0
        self.pending = []

    def slot(self):
        self.used += 1
        return self.used - 1

    def make(self, src, dst, device, slot):
        return pltpu.make_async_remote_copy(
            src_ref=src,
            dst_ref=dst,
            send_sem=self.send_sem.at[slot],
            recv_sem=self.recv_sem.at[slot],
            device_id=device,
            device_id_type=MESH,
        )

    def send(self, src, dst, device, slot=None, unless=None):
        slot = self.slot() if slot is None else slot
        copy = self.make(src, dst, device, slot)
        if unless is None:
            copy.start()
        else:
            pl.when(jnp.logical_not(unless))(copy.start)
        self.pending.append((copy, unless))
        return slot

    def arrived(self, ref, device, slot, unless=None):
        copy = self.make(ref, ref, device, slot)
        if unless is None:
            copy.wait_recv()
        else:
            pl.when(jnp.logical_not(unless))(copy.wait_recv)

    def drain(self):
        for copy, unless in self.pending:
            if unless is None:
                copy.wait_send()
            else:
                pl.when(jnp.logical_not(unless))(copy.wait_send)
        self.pending = []


def kernel(
    a_ref,
    pattern_ref,
    panel1_ref,
    panel2_ref,
    rows1_ref,
    rows2_ref,
    inner_ref,
    c1_ref,
    c2_ref,
    xg0,
    xg1,
    ao,
    ax,
    pattern,
    panels,
    rows,
    inner,
    xt,
    pt,
    ptx,
    mx,
    t,
    town,
    rxd,
    rx,
    s1,
    s1own,
    rzd,
    rz,
    g,
    part0,
    recv0,
    back0,
    part1,
    recv1,
    back1,
    send_sem,
    recv_sem,
    local_sem,
):
    r = lax.axis_index("prow")
    c = lax.axis_index("pcol")
    y = r % NY
    zl = r // NY
    zh = c // 8
    x = (c // 2) % NX
    core = c % 2
    j = c % 8
    z = zh * 2 + zl

    def at(yy=None, zz=None, xx=None, cc=None):
        yy = y if yy is None else yy
        zz = z if zz is None else zz
        xx = x if xx is None else xx
        cc = core if cc is None else cc
        return ((zz % 2) * NY + yy, (zz // 2) * 8 + xx * 2 + cc)

    mate = at(cc=1 - core)
    xn, xp = at(xx=(x + 1) % NX), at(xx=(x + 3) % NX)
    zhn, zhp = at(zz=(z + 2) % 8), at(zz=(z + 6) % 8)
    yn, yp = at(yy=(y + 1) % NY), at(yy=(y + 3) % NY)
    zmate = at(zz=zh * 2 + 1 - zl)
    diag_n, diag_p = at(yy=(y + 1) % NY, zz=zh * 2 + 1 - zl), at(yy=(y + 3) % NY, zz=zh * 2 + 1 - zl)

    def yz_peer(e):
        return (y + e // 8) % NY, (z + e % 8) % 8

    barrier = pltpu.get_barrier_semaphore()
    first_self = c // 4 == r
    own_self = (c // 4 == r) & (8 * (c % 4) + r == c)
    for device in [mate, xn, xp]:
        pl.semaphore_signal(barrier, inc=1, device_id=device, device_id_type=MESH)

    def greet(e, _):
        peer_y, peer_z = yz_peer(e)
        pl.semaphore_signal(
            barrier, inc=1, device_id=at(yy=peer_y, zz=peer_z), device_id_type=MESH
        )
        return 0

    lax.fori_loop(1, 32, greet, 0)
    for i in range(4):

        @pl.when(jnp.logical_not(first_self & (c % 4 == i)))
        def _():
            pl.semaphore_signal(barrier, inc=1, device_id=(c // 4, 4 * r + i), device_id_type=MESH)

    @pl.when(jnp.logical_not(own_self))
    def _():
        pl.semaphore_signal(barrier, inc=1, device_id=(j, 4 * r + zh), device_id_type=MESH)

    own_rows = pl.ds(pl.multiple_of(24 * r, 8), 24)
    loads = [
        pltpu.make_async_copy(rows1_ref.at[own_rows], rows.at[0], local_sem.at[3]),
        pltpu.make_async_copy(rows2_ref.at[own_rows], rows.at[1], local_sem.at[4]),
        pltpu.make_async_copy(panel1_ref, panels.at[0], local_sem.at[5]),
        pltpu.make_async_copy(panel2_ref, panels.at[1], local_sem.at[6]),
        pltpu.make_async_copy(pattern_ref, pattern, local_sem.at[7]),
        pltpu.make_async_copy(a_ref.at[:, :, core], ao, local_sem.at[0]),
        pltpu.make_async_copy(inner_ref, inner, local_sem.at[8]),
    ]
    for load in loads:
        load.start()
    for load in loads[:4]:
        load.wait()
    keep1 = rows[0].astype(F32)
    keep2 = keep1 * rows[1].astype(F32)
    for p, keep in enumerate((keep1, keep2)):
        for k in range(24):
            cut = slice(128 * k, 128 * k + 128)
            xt[p, :, cut] = (panels[p, :, cut].astype(F32) * keep[k : k + 1]).astype(BF16)

    pl.semaphore_wait(
        barrier, 34 + 5 - first_self.astype(jnp.int32) - own_self.astype(jnp.int32)
    )

    links = Links(send_sem, recv_sem)

    slice16 = pl.ds(pl.multiple_of(16 * (c % 4), 16), 16)
    base_first = [links.slot() for _ in range(8)][0]
    own_slot = links.slot()

    def spread(source, target, base, device, me, q, spare):
        copy = pltpu.make_async_remote_copy(
            src_ref=source,
            dst_ref=target,
            send_sem=send_sem.at[base + q],
            recv_sem=recv_sem.at[base + c % 4],
            device_id=device,
            device_id_type=MESH,
        )
        pl.when(jnp.logical_not(me))(copy.start)
        links.pending.append((copy, me))

        @pl.when(me)
        def _():
            local = pltpu.make_async_copy(source, target, local_sem.at[spare])
            local.start()
            local.wait()

    for p in range(2):
        for q in range(4):
            spread(
                xt.at[p, :, pl.ds(768 * q, 768)],
                pt.at[c // 4, p, slice16, :],
                base_first + 4 * p,
                (c // 4, 4 * r + q),
                first_self & (c % 4 == q),
                q,
                1,
            )

    a_slot = links.send(a_ref.at[:, :, 1 - core], ax, mate)

    def send_own_rows():
        links.send(pt.at[r], mx, (c // 4, 8 * (c % 4) + r), own_slot, own_self)

        @pl.when(own_self)
        def _():
            local = pltpu.make_async_copy(pt.at[r], mx, local_sem.at[2])
            local.start()
            local.wait()

    def mask_rows(ref, owner):
        def chunk(i, _):
            m = i // NX
            n = i % NX
            for k in range(2):
                cut = slice(TILE * k, TILE * k + TILE)
                keep = pattern[8 * r + 2 * m + n // 2, 2 * owner + k].astype(F32)
                ref[m, n, :, cut] = (ref[m, n, :, cut].astype(F32) * keep).astype(BF16)
            return 0

        lax.fori_loop(0, NZH * NX, chunk, 0)

    for load in loads[4:]:
        load.wait()
    mask_rows(ao, c)

    def row_of(yy, zz):
        return zz * NY + yy

    r_z = row_of(y, 1 - zl)
    y_p, y_n, y_d = (y + 3) % NY, (y + 1) % NY, (y + 2) % NY

    def panel_gather(p):
        forwarded = []

        def to(device, row):
            return links.send(pt.at[row, p], pt.at[row, p], device)

        def to_mate(row):
            forwarded.append((row, links.send(pt.at[row, p], ptx.at[row, p], mate)))

        def part(row, h):
            return pt.at[row, p, pl.ds(32 * h, 32)]

        for i in range(4):
            links.arrived(
                pt.at[r, p, pl.ds(16 * i, 16), :],
                mate,
                base_first + 4 * p + i,
                first_self & (c % 4 == i),
            )
        got_yp, got_yn = to(yn, r), to(yp, r)
        got_diag_p, got_diag_n = to(diag_n, r), to(diag_p, r)
        got_z = to(zmate, r)
        to_mate(r)
        yield
        relayed = []
        arrivals = ((zl, got_yp, got_yn, yp, yn), (1 - zl, got_diag_p, got_diag_n, diag_p, diag_n))
        for zz, slot_p, slot_n, from_p, from_n in arrivals:
            row_p, row_n, row_d = row_of(y_p, zz), row_of(y_n, zz), row_of(y_d, zz)
            links.arrived(pt.at[row_p, p], from_p, slot_p)
            got_d0 = links.send(part(row_p, 0), part(row_p, 0), yn)
            links.arrived(pt.at[row_n, p], from_n, slot_n)
            got_d1 = links.send(part(row_n, 1), part(row_n, 1), yp)
            to_mate(row_p)
            to_mate(row_n)
            relayed.append((row_d, got_d0, got_d1))
        links.arrived(pt.at[r_z, p], zmate, got_z)
        to_mate(r_z)
        yield
        for row_d, got_d0, got_d1 in relayed:
            links.arrived(part(row_d, 0), yp, got_d0)
            links.arrived(part(row_d, 1), yn, got_d1)
            to_mate(row_d)
        yield
        for row, slot in forwarded:
            links.arrived(ptx.at[row, p], mate, slot)
        yield

    def product(p, xx, out):
        left = ao[:, xx].reshape(NZH * SHARE, BLOCK)
        left_x = ax[:, xx].reshape(NZH * SHARE, BLOCK)
        for h in range(2):
            right = pt[pl.ds(4 * h, 4), p].reshape(256, BLOCK)
            right_x = ptx[pl.ds(4 * h, 4), p].reshape(256, BLOCK)
            value = nt_dot(left, right) + nt_dot(left_x, right_x)
            out[..., pl.ds(256 * h, 256)] = value.reshape(NZH, SHARE, 256).astype(out.dtype)

    half = SHARE // 2
    lo, hi = pl.ds(0, half), pl.ds(half, half)
    zh_n, zh_p, zh_d = (zh + 1) % NZH, (zh + 3) % NZH, (zh + 2) % NZH
    jn, jp, jd = (j + 2) % 8, (j + 6) % 8, (j + 4) % 8

    def over_x_core(buf, part):
        own_p = links.send(buf(j), buf(j), xn)
        own_n = links.send(buf(j), buf(j), xp)
        own_m = links.send(buf(j), buf(j), mate)
        yield
        links.arrived(buf(jp), xp, own_p)
        d0 = links.send(part(jp, 0), part(jp, 0), xn)
        links.arrived(buf(jn), xn, own_n)
        d1 = links.send(part(jn, 1), part(jn, 1), xp)
        m_p = links.send(buf(jp), buf(jp), mate)
        m_n = links.send(buf(jn), buf(jn), mate)
        yield
        links.arrived(part(jd, 0), xp, d0)
        links.arrived(part(jd, 1), xn, d1)
        m_d = links.send(buf(jd), buf(jd), mate)
        yield
        other = 1 - 2 * core
        links.arrived(buf(j + other), mate, own_m)
        links.arrived(buf(jp + other), mate, m_p)
        links.arrived(buf(jn + other), mate, m_n)
        links.arrived(buf(jd + other), mate, m_d)

    def chain(p):
        product(p, (x + 2) % NX, t.at[p, 0])
        got_p = links.send(t.at[p, 0, pl.ds(0, 2)], rxd.at[p, 0], xn)
        got_n = links.send(t.at[p, 0, pl.ds(2, 2)], rxd.at[p, 1], xp)
        yield
        product(p, (x + 1) % NX, t.at[p, 1])
        pure_p = links.send(t.at[p, 1, pl.ds(2, 2)], rx.at[p, 0, pl.ds(2, 2)], xn)
        yield
        product(p, (x + 3) % NX, t.at[p, 2])
        pure_n = links.send(t.at[p, 2, pl.ds(0, 2)], rx.at[p, 1, pl.ds(0, 2)], xp)
        yield
        links.arrived(rxd.at[p, 0], xp, got_p)
        t[p, 1, 0:2] = (t[p, 1, 0:2].astype(F32) + rxd[p, 0].astype(F32)).astype(BF16)
        sum_p = links.send(t.at[p, 1, pl.ds(0, 2)], rx.at[p, 0, pl.ds(0, 2)], xn)
        links.arrived(rxd.at[p, 1], xn, got_n)
        t[p, 2, 2:4] = (t[p, 2, 2:4].astype(F32) + rxd[p, 1].astype(F32)).astype(BF16)
        sum_n = links.send(t.at[p, 2, pl.ds(2, 2)], rx.at[p, 1, pl.ds(2, 2)], xp)
        yield
        product(p, x, town.at[p])
        yield
        links.arrived(rx.at[p, 0, pl.ds(2, 2)], xp, pure_p)
        links.arrived(rx.at[p, 1, pl.ds(0, 2)], xn, pure_n)
        links.arrived(rx.at[p, 0, pl.ds(0, 2)], xp, sum_p)
        links.arrived(rx.at[p, 1, pl.ds(2, 2)], xn, sum_n)

        def total(k):
            return town[p, k] + rx[p, 0, k].astype(F32) + rx[p, 1, k].astype(F32)

        s1[p, 0] = total(zh_d).astype(BF16)
        got_p = links.send(s1.at[p, 0, lo], rzd.at[p, 0], zhn)
        got_n = links.send(s1.at[p, 0, hi], rzd.at[p, 1], zhp)
        s1[p, 1] = total(zh_n).astype(BF16)
        pure_p = links.send(s1.at[p, 1, hi], rz.at[p, 0, hi], zhn)
        s1[p, 2] = total(zh_p).astype(BF16)
        pure_n = links.send(s1.at[p, 2, lo], rz.at[p, 1, lo], zhp)
        s1own[p] = total(zh)
        yield
        links.arrived(rzd.at[p, 0], zhp, got_p)
        s1[p, 1, lo] = (s1[p, 1, lo].astype(F32) + rzd[p, 0].astype(F32)).astype(BF16)
        sum_p = links.send(s1.at[p, 1, lo], rz.at[p, 0, lo], zhn)
        links.arrived(rzd.at[p, 1], zhn, got_n)
        s1[p, 2, hi] = (s1[p, 2, hi].astype(F32) + rzd[p, 1].astype(F32)).astype(BF16)
        sum_n = links.send(s1.at[p, 2, hi], rz.at[p, 1, hi], zhp)
        yield
        links.arrived(rz.at[p, 0, hi], zhp, pure_p)
        links.arrived(rz.at[p, 1, lo], zhn, pure_n)
        links.arrived(rz.at[p, 0, lo], zhp, sum_p)
        links.arrived(rz.at[p, 1, hi], zhn, sum_n)
        total_sum = s1own[p] + rz[p, 0].astype(F32) + rz[p, 1].astype(F32)
        if p == 0:
            column = (-total_sum).astype(BF16)
            c1_ref[...] = column
        else:
            column = (-(total_sum + nn_dot(c1_ref[...], inner[...]))).astype(BF16)
            c2_ref[...] = column
        g[p, j] = column
        yield from over_x_core(
            lambda k: g.at[p, k], lambda k, h: g.at[p, k, pl.ds(half * h, half)]
        )

        if p == 0:
            links.arrived(mx, mate, own_slot, own_self)
        sides = (0, 1) if p == 0 else (1,)
        n = 64 * len(sides)
        xg, part, recv, back = ((xg0, part0, recv0, back0), (xg1, part1, recv1, back1))[p]
        for k, m in enumerate(sides):
            found = nn_dot(mx[m], g[p].reshape(BLOCK, W))
            for d in range(NY):
                rows = found[:, 128 * d : 128 * d + 128]
                step = n // 8
                part[d, pl.ds(64 // step * k, 64 // step)] = rows.reshape(
                    64 // step, step, 128
                ).astype(part.dtype)
        out_slot, back_slot = links.slot(), links.slot()

        def to_all(copy_of):
            def start(e, _):
                copy_of(e).start()
                return 0

            lax.fori_loop(1, 32, start, 0)

        def piece(e):
            peer_y, peer_z = yz_peer(e)
            return links.make(
                part.at[peer_y, peer_z], recv.at[e - 1], at(yy=peer_y, zz=peer_z), out_slot
            )

        to_all(piece)
        every = links.make(recv, recv, mate, out_slot)
        links.pending.append((every, None))
        yield
        every.wait_recv()
        total_yz = part[y, z].astype(F32)
        for e in range(1, 32):
            total_yz = total_yz + recv[e - 1].astype(F32)
        back[y, z] = total_yz.astype(back.dtype)

        def reply(e):
            peer_y, peer_z = yz_peer(e)
            return links.make(
                back.at[y, z], back.at[y, z], at(yy=peer_y, zz=peer_z), back_slot
            )

        to_all(reply)
        every = links.make(recv, recv, mate, back_slot)
        links.pending.append((every, None))
        yield
        every.wait_recv()
        xg[j] = back[...].reshape(NY, n, 128).astype(BF16)
        yield from over_x_core(lambda k: xg.at[k], lambda k, h: xg.at[k, pl.ds(2 * h, 2)])
        yield

    parts = {
        "f": panel_gather(0),
        "s": panel_gather(1),
        "A": chain(0),
        "B": chain(1),
    }
    for name in ORDER:
        if name == "m":
            links.arrived(ax, mate, a_slot)
            mask_rows(ax, c + 1 - 2 * core)
        elif name == "o":
            send_own_rows()
        else:
            next(parts[name])
    links.drain()


ORDER = "mfsoffsf" + "AsAAAsA" + "BBBA" + "BABAAB" + "AABBABBABABABABBB"
N_COPIES = 128


def finish(
        inner_ref,
    pivot1_ref,
    pivot2_ref,
    xg0,
    xg1,
    c1_ref,
    c2_ref,
    d1_out,
    i2_out,
    d2_out,
    c1_out,
    c2_out,
    d1,
    i2,
    d2,
    crossed,
    sem,
):
    def assemble(out, source, first, pivot):
        for k in range(8):
            for d in range(NY):
                rows, cols = slice(64 * k, 64 * k + 64), slice(128 * d, 128 * d + 128)
                part = source[k, d, first : first + 64].astype(F32)
                out[rows, cols] = part if pivot is None else pivot[rows, cols] - part

    def parts_dot(dot, wide):
        high = wide.astype(BF16)
        low = (wide - high.astype(F32)).astype(BF16)
        return dot(high) + dot(low)

    copies = [
        pltpu.make_async_copy(c1_ref, c1_out, sem.at[3]),
        pltpu.make_async_copy(c2_ref, c2_out, sem.at[4]),
        pltpu.make_async_copy(d1, d1_out, sem.at[0]),
        pltpu.make_async_copy(i2, i2_out, sem.at[1]),
        pltpu.make_async_copy(d2, d2_out, sem.at[2]),
    ]
    copies[0].start()
    copies[1].start()
    inner = inner_ref[...]
    assemble(d1, xg0, 0, pivot1_ref)
    copies[2].start()
    assemble(crossed, xg0, 64, None)
    i2[...] = -(parts_dot(lambda v: nn_dot(v, inner), d1[...]) + crossed[...].T)
    copies[3].start()
    inner_t = inner.T
    assemble(d2, xg1, 0, pivot2_ref)
    d2[...] = d2[...] - parts_dot(lambda v: nn_dot(inner_t, v), i2[...])
    copies[4].start()
    for copy in copies:
        copy.wait()


def body(
    ancestor_inverse,
    tile_pattern,
    rows_first,
    rows_second,
    panel_first,
    panel_second,
    inner_panel,
    pivot_first,
    pivot_second,
):
    col_block = ancestor_inverse.shape[1]
    halves = ancestor_inverse.reshape(NZH, NX, NC, SHARE, col_block)
    anywhere = pl.BlockSpec(memory_space=pl.ANY)
    in_hbm = pl.BlockSpec(memory_space=pltpu.HBM)
    vmem = pl.BlockSpec(memory_space=pltpu.VMEM)
    wide = jax.ShapeDtypeStruct((W, W), F32)
    column_first, column_second, gathered0, gathered1 = pl.pallas_call(
        kernel,
        out_shape=(
            jax.ShapeDtypeStruct((SHARE, W), BF16),
            jax.ShapeDtypeStruct((SHARE, W), BF16),
            jax.ShapeDtypeStruct((8, NY, 128, 128), BF16),
            jax.ShapeDtypeStruct((8, NY, 64, 128), BF16),
        ),
        in_specs=[in_hbm] * 7,
        out_specs=(vmem, vmem, vmem, vmem),
        scratch_shapes=[
            pltpu.VMEM((NZH, NX, SHARE, BLOCK), BF16),
            pltpu.VMEM((NZH, NX, SHARE, BLOCK), BF16),
            pltpu.SMEM((64, 64), jnp.int32),
            pltpu.VMEM((2, 16, 3072), BF16),
            pltpu.VMEM((2, 24, 128), jnp.int32),
            pltpu.VMEM((W, W), BF16),
            pltpu.VMEM((2, 16, 3072), BF16),
            pltpu.VMEM((8, 2, 64, BLOCK), BF16),
            pltpu.VMEM((8, 2, 64, BLOCK), BF16),
            pltpu.VMEM((2, 64, BLOCK), BF16),
            pltpu.VMEM((2, 3, NZH, SHARE, W), BF16),
            pltpu.VMEM((2, NZH, SHARE, W), F32),
            pltpu.VMEM((2, 2, 2, SHARE, W), BF16),
            pltpu.VMEM((2, 2, NZH, SHARE, W), BF16),
            pltpu.VMEM((2, 3, SHARE, W), BF16),
            pltpu.VMEM((2, SHARE, W), F32),
            pltpu.VMEM((2, 2, SHARE // 2, W), BF16),
            pltpu.VMEM((2, 2, SHARE, W), BF16),
            pltpu.VMEM((2, 8, SHARE, W), BF16),
            pltpu.VMEM((NY, 8, 16, 128), BF16),
            pltpu.VMEM((31, 16, 128), BF16),
            pltpu.VMEM((NY, 8, 16, 128), BF16),
            pltpu.VMEM((NY, 8, 8, 128), F32),
            pltpu.VMEM((31, 8, 128), F32),
            pltpu.VMEM((NY, 8, 8, 128), F32),
            pltpu.SemaphoreType.DMA((N_COPIES,)),
            pltpu.SemaphoreType.DMA((N_COPIES,)),
            pltpu.SemaphoreType.DMA((9,)),
        ],
        compiler_params=pltpu.CompilerParams(
            collective_id=0, has_side_effects=True, vmem_limit_bytes=48 * 2**20
        ),
    )(
        *(
            pltpu.with_memory_space_constraint(array, pltpu.HBM)
            for array in (
                halves,
                tile_pattern,
                panel_first.T,
                panel_second.T,
                rows_first.reshape(-1, 128),
                rows_second.reshape(-1, 128),
                inner_panel,
            )
        )
    )
    narrow = jax.ShapeDtypeStruct((SHARE, W), BF16)
    diagonal_first, inner_second, diagonal_second, column_first, column_second = pl.pallas_call(
        finish,
        out_shape=(wide, wide, wide, narrow, narrow),
        in_specs=[vmem] * 7,
        out_specs=(anywhere,) * 5,
        scratch_shapes=[pltpu.VMEM((W, W), F32)] * 4 + [pltpu.SemaphoreType.DMA((5,))],
        compiler_params=pltpu.CompilerParams(vmem_limit_bytes=32 * 2**20),
    )(
        inner_panel, pivot_first, pivot_second, gathered0, gathered1, column_first, column_second
    )
    return (column_first, diagonal_first, inner_second, column_second, diagonal_second)


def solution(mesh):
    return jax.shard_map(
        body,
        mesh=mesh,
        in_specs=(
            P("prow", "pcol"),
            P(),
            P(),
            P(),
            P("prow", "pcol"),
            P("prow", "pcol"),
            P(),
            P(),
            P(),
        ),
        out_specs=(P(("prow", "pcol"), None), P(), P(), P(("prow", "pcol"), None), P()),
        check_vma=False,
    )
```

```python
import jax
import jax.numpy as jnp
from jax import lax
from jax.experimental import pallas as pl
from jax.experimental.pallas import tpu as pltpu
from jax.sharding import PartitionSpec as P

TILE = 384
MESH = pl.DeviceIdType.MESH
BF16 = jnp.bfloat16
F32 = jnp.float32

NY, NX, NZH, NZL, NC = 4, 4, 4, 2, 2
BLOCK = 768
SHARE = 96
W = 512


def nt_dot(left, right):
    return lax.dot_general(left, right, (((1,), (1,)), ((), ())), preferred_element_type=F32)


def nn_dot(left, right):
    return jnp.dot(left, right, preferred_element_type=F32)


class Links:
    def __init__(self, send_sem, recv_sem):
        self.send_sem = send_sem
        self.recv_sem = recv_sem
        self.used = 0
        self.pending = []

    def slot(self):
        self.used += 1
        return self.used - 1

    def make(self, src, dst, device, slot):
        return pltpu.make_async_remote_copy(
            src_ref=src,
            dst_ref=dst,
            send_sem=self.send_sem.at[slot],
            recv_sem=self.recv_sem.at[slot],
            device_id=device,
            device_id_type=MESH,
        )

    def send(self, src, dst, device, slot=None, unless=None):
        slot = self.slot() if slot is None else slot
        copy = self.make(src, dst, device, slot)
        if unless is None:
            copy.start()
        else:
            pl.when(jnp.logical_not(unless))(copy.start)
        self.pending.append((copy, unless))
        return slot

    def arrived(self, ref, device, slot, unless=None):
        copy = self.make(ref, ref, device, slot)
        if unless is None:
            copy.wait_recv()
        else:
            pl.when(jnp.logical_not(unless))(copy.wait_recv)

    def drain(self):
        for copy, unless in self.pending:
            if unless is None:
                copy.wait_send()
            else:
                pl.when(jnp.logical_not(unless))(copy.wait_send)
        self.pending = []


def kernel(
    a_ref,
    pattern_ref,
    panel1_ref,
    panel2_ref,
    rows1_ref,
    rows2_ref,
    inner_ref,
    c1_ref,
    c2_ref,
    xg0,
    xg1,
    ao,
    ax,
    pattern,
    panels,
    rows,
    inner,
    xt,
    pt,
    ptx,
    mx,
    t,
    town,
    rxd,
    rx,
    s1,
    s1own,
    rzd,
    rz,
    g,
    part0,
    recv0,
    back0,
    part1,
    recv1,
    back1,
    send_sem,
    recv_sem,
    local_sem,
):
    r = lax.axis_index("prow")
    c = lax.axis_index("pcol")
    y = r % NY
    zl = r // NY
    zh = c // 8
    x = (c // 2) % NX
    core = c % 2
    j = c % 8
    z = zh * 2 + zl

    def at(yy=None, zz=None, xx=None, cc=None):
        yy = y if yy is None else yy
        zz = z if zz is None else zz
        xx = x if xx is None else xx
        cc = core if cc is None else cc
        return ((zz % 2) * NY + yy, (zz // 2) * 8 + xx * 2 + cc)

    mate = at(cc=1 - core)
    xn, xp = at(xx=(x + 1) % NX), at(xx=(x + 3) % NX)
    zhn, zhp = at(zz=(z + 2) % 8), at(zz=(z + 6) % 8)
    yn, yp = at(yy=(y + 1) % NY), at(yy=(y + 3) % NY)
    zmate = at(zz=zh * 2 + 1 - zl)
    def yz_peer(e):
        return (y + e // 8) % NY, (z + e % 8) % 8

    barrier = pltpu.get_barrier_semaphore()
    first_self = c // 4 == r
    own_self = (c // 4 == r) & (8 * (c % 4) + r == c)
    for device in [mate, xn, xp]:
        pl.semaphore_signal(barrier, inc=1, device_id=device, device_id_type=MESH)

    def greet(e, _):
        peer_y, peer_z = yz_peer(e)
        pl.semaphore_signal(
            barrier, inc=1, device_id=at(yy=peer_y, zz=peer_z), device_id_type=MESH
        )
        return 0

    lax.fori_loop(1, 32, greet, 0)
    for i in range(4):

        @pl.when(jnp.logical_not(first_self & (c % 4 == i)))
        def _():
            pl.semaphore_signal(barrier, inc=1, device_id=(c // 4, 4 * r + i), device_id_type=MESH)

    @pl.when(jnp.logical_not(own_self))
    def _():
        pl.semaphore_signal(barrier, inc=1, device_id=(j, 4 * r + zh), device_id_type=MESH)

    own_rows = pl.ds(pl.multiple_of(24 * r, 8), 24)
    loads = [
        pltpu.make_async_copy(rows1_ref.at[own_rows], rows.at[0], local_sem.at[3]),
        pltpu.make_async_copy(rows2_ref.at[own_rows], rows.at[1], local_sem.at[4]),
        pltpu.make_async_copy(panel1_ref, panels.at[0], local_sem.at[5]),
        pltpu.make_async_copy(panel2_ref, panels.at[1], local_sem.at[6]),
        pltpu.make_async_copy(pattern_ref, pattern, local_sem.at[7]),
        pltpu.make_async_copy(a_ref.at[:, :, core], ao, local_sem.at[0]),
        pltpu.make_async_copy(inner_ref, inner, local_sem.at[8]),
    ]
    for load in loads:
        load.start()
    for load in loads[:4]:
        load.wait()
    keep1 = rows[0].astype(F32)
    keep2 = keep1 * rows[1].astype(F32)
    for p, keep in enumerate((keep1, keep2)):
        for k in range(24):
            cut = slice(128 * k, 128 * k + 128)
            xt[p, :, cut] = (panels[p, :, cut].astype(F32) * keep[k : k + 1]).astype(BF16)

    pl.semaphore_wait(
        barrier, 34 + 5 - first_self.astype(jnp.int32) - own_self.astype(jnp.int32)
    )

    links = Links(send_sem, recv_sem)

    slice16 = pl.ds(pl.multiple_of(16 * (c % 4), 16), 16)
    base_first = [links.slot() for _ in range(8)][0]
    own_slot = links.slot()

    def spread(source, target, base, device, me, q, spare):
        copy = pltpu.make_async_remote_copy(
            src_ref=source,
            dst_ref=target,
            send_sem=send_sem.at[base + q],
            recv_sem=recv_sem.at[base + c % 4],
            device_id=device,
            device_id_type=MESH,
        )
        pl.when(jnp.logical_not(me))(copy.start)
        links.pending.append((copy, me))

        @pl.when(me)
        def _():
            local = pltpu.make_async_copy(source, target, local_sem.at[spare])
            local.start()
            local.wait()

    for p in range(2):
        for q in range(4):
            spread(
                xt.at[p, :, pl.ds(768 * q, 768)],
                pt.at[c // 4, p, slice16, :],
                base_first + 4 * p,
                (c // 4, 4 * r + q),
                first_self & (c % 4 == q),
                q,
                1,
            )

    a_slot = links.send(a_ref.at[:, :, 1 - core], ax, mate)

    def send_own_rows():
        links.send(pt.at[r], mx, (c // 4, 8 * (c % 4) + r), own_slot, own_self)

        @pl.when(own_self)
        def _():
            local = pltpu.make_async_copy(pt.at[r], mx, local_sem.at[2])
            local.start()
            local.wait()

    def mask_rows(ref, owner):
        def chunk(i, _):
            m = i // NX
            n = i % NX
            for k in range(2):
                cut = slice(TILE * k, TILE * k + TILE)
                keep = pattern[8 * r + 2 * m + n // 2, 2 * owner + k].astype(F32)
                ref[m, n, :, cut] = (ref[m, n, :, cut].astype(F32) * keep).astype(BF16)
            return 0

        lax.fori_loop(0, NZH * NX, chunk, 0)

    for load in loads[4:]:
        load.wait()
    mask_rows(ao, c)

    def row_of(yy, zz):
        return zz * NY + yy

    r_z = row_of(y, 1 - zl)
    y_p, y_n, y_d = (y + 3) % NY, (y + 1) % NY, (y + 2) % NY

    def panel_gather(p):
        forwarded = []

        def to(device, row):
            return links.send(pt.at[row, p], pt.at[row, p], device)

        def to_mate(row):
            forwarded.append((row, links.send(pt.at[row, p], ptx.at[row, p], mate)))

        def part(row, h):
            return pt.at[row, p, pl.ds(32 * h, 32)]

        for i in range(4):
            links.arrived(
                pt.at[r, p, pl.ds(16 * i, 16), :],
                mate,
                base_first + 4 * p + i,
                first_self & (c % 4 == i),
            )
        got_z, got_yp, got_yn = to(zmate, r), to(yn, r), to(yp, r)
        to_mate(r)
        yield
        links.arrived(pt.at[r_z, p], zmate, got_z)
        got_yp_z, got_yn_z = to(yn, r_z), to(yp, r_z)
        to_mate(r_z)
        yield
        relayed = []
        for zz, slot_p, slot_n in ((zl, got_yp, got_yn), (1 - zl, got_yp_z, got_yn_z)):
            row_p, row_n, row_d = row_of(y_p, zz), row_of(y_n, zz), row_of(y_d, zz)
            links.arrived(pt.at[row_p, p], yp, slot_p)
            got_d0 = links.send(part(row_p, 0), part(row_p, 0), yn)
            links.arrived(pt.at[row_n, p], yn, slot_n)
            got_d1 = links.send(part(row_n, 1), part(row_n, 1), yp)
            to_mate(row_p)
            to_mate(row_n)
            relayed.append((row_d, got_d0, got_d1))
            yield
        for row_d, got_d0, got_d1 in relayed:
            links.arrived(part(row_d, 0), yp, got_d0)
            links.arrived(part(row_d, 1), yn, got_d1)
            to_mate(row_d)
        yield
        for row, slot in forwarded:
            links.arrived(ptx.at[row, p], mate, slot)
        yield

    def product(p, xx, out):
        left = ao[:, xx].reshape(NZH * SHARE, BLOCK)
        left_x = ax[:, xx].reshape(NZH * SHARE, BLOCK)
        for h in range(2):
            right = pt[pl.ds(4 * h, 4), p].reshape(256, BLOCK)
            right_x = ptx[pl.ds(4 * h, 4), p].reshape(256, BLOCK)
            value = nt_dot(left, right) + nt_dot(left_x, right_x)
            out[..., pl.ds(256 * h, 256)] = value.reshape(NZH, SHARE, 256).astype(out.dtype)

    half = SHARE // 2
    lo, hi = pl.ds(0, half), pl.ds(half, half)
    zh_n, zh_p, zh_d = (zh + 1) % NZH, (zh + 3) % NZH, (zh + 2) % NZH
    jn, jp, jd = (j + 2) % 8, (j + 6) % 8, (j + 4) % 8

    def over_x_core(buf, part):
        own_p = links.send(buf(j), buf(j), xn)
        own_n = links.send(buf(j), buf(j), xp)
        own_m = links.send(buf(j), buf(j), mate)
        yield
        links.arrived(buf(jp), xp, own_p)
        d0 = links.send(part(jp, 0), part(jp, 0), xn)
        links.arrived(buf(jn), xn, own_n)
        d1 = links.send(part(jn, 1), part(jn, 1), xp)
        m_p = links.send(buf(jp), buf(jp), mate)
        m_n = links.send(buf(jn), buf(jn), mate)
        yield
        links.arrived(part(jd, 0), xp, d0)
        links.arrived(part(jd, 1), xn, d1)
        m_d = links.send(buf(jd), buf(jd), mate)
        yield
        other = 1 - 2 * core
        links.arrived(buf(j + other), mate, own_m)
        links.arrived(buf(jp + other), mate, m_p)
        links.arrived(buf(jn + other), mate, m_n)
        links.arrived(buf(jd + other), mate, m_d)

    def chain(p):
        product(p, (x + 2) % NX, t.at[p, 0])
        got_p = links.send(t.at[p, 0, pl.ds(0, 2)], rxd.at[p, 0], xn)
        got_n = links.send(t.at[p, 0, pl.ds(2, 2)], rxd.at[p, 1], xp)
        yield
        product(p, (x + 1) % NX, t.at[p, 1])
        pure_p = links.send(t.at[p, 1, pl.ds(2, 2)], rx.at[p, 0, pl.ds(2, 2)], xn)
        yield
        product(p, (x + 3) % NX, t.at[p, 2])
        pure_n = links.send(t.at[p, 2, pl.ds(0, 2)], rx.at[p, 1, pl.ds(0, 2)], xp)
        yield
        links.arrived(rxd.at[p, 0], xp, got_p)
        t[p, 1, 0:2] = (t[p, 1, 0:2].astype(F32) + rxd[p, 0].astype(F32)).astype(BF16)
        sum_p = links.send(t.at[p, 1, pl.ds(0, 2)], rx.at[p, 0, pl.ds(0, 2)], xn)
        links.arrived(rxd.at[p, 1], xn, got_n)
        t[p, 2, 2:4] = (t[p, 2, 2:4].astype(F32) + rxd[p, 1].astype(F32)).astype(BF16)
        sum_n = links.send(t.at[p, 2, pl.ds(2, 2)], rx.at[p, 1, pl.ds(2, 2)], xp)
        yield
        product(p, x, town.at[p])
        yield
        links.arrived(rx.at[p, 0, pl.ds(2, 2)], xp, pure_p)
        links.arrived(rx.at[p, 1, pl.ds(0, 2)], xn, pure_n)
        links.arrived(rx.at[p, 0, pl.ds(0, 2)], xp, sum_p)
        links.arrived(rx.at[p, 1, pl.ds(2, 2)], xn, sum_n)

        def total(k):
            return town[p, k] + rx[p, 0, k].astype(F32) + rx[p, 1, k].astype(F32)

        s1[p, 0] = total(zh_d).astype(BF16)
        got_p = links.send(s1.at[p, 0, lo], rzd.at[p, 0], zhn)
        got_n = links.send(s1.at[p, 0, hi], rzd.at[p, 1], zhp)
        s1[p, 1] = total(zh_n).astype(BF16)
        pure_p = links.send(s1.at[p, 1, hi], rz.at[p, 0, hi], zhn)
        s1[p, 2] = total(zh_p).astype(BF16)
        pure_n = links.send(s1.at[p, 2, lo], rz.at[p, 1, lo], zhp)
        s1own[p] = total(zh)
        yield
        links.arrived(rzd.at[p, 0], zhp, got_p)
        s1[p, 1, lo] = (s1[p, 1, lo].astype(F32) + rzd[p, 0].astype(F32)).astype(BF16)
        sum_p = links.send(s1.at[p, 1, lo], rz.at[p, 0, lo], zhn)
        links.arrived(rzd.at[p, 1], zhn, got_n)
        s1[p, 2, hi] = (s1[p, 2, hi].astype(F32) + rzd[p, 1].astype(F32)).astype(BF16)
        sum_n = links.send(s1.at[p, 2, hi], rz.at[p, 1, hi], zhp)
        yield
        links.arrived(rz.at[p, 0, hi], zhp, pure_p)
        links.arrived(rz.at[p, 1, lo], zhn, pure_n)
        links.arrived(rz.at[p, 0, lo], zhp, sum_p)
        links.arrived(rz.at[p, 1, hi], zhn, sum_n)
        total_sum = s1own[p] + rz[p, 0].astype(F32) + rz[p, 1].astype(F32)
        if p == 0:
            column = (-total_sum).astype(BF16)
            c1_ref[...] = column
        else:
            column = (-(total_sum + nn_dot(c1_ref[...], inner[...]))).astype(BF16)
            c2_ref[...] = column
        g[p, j] = column
        yield from over_x_core(
            lambda k: g.at[p, k], lambda k, h: g.at[p, k, pl.ds(half * h, half)]
        )

        if p == 0:
            links.arrived(mx, mate, own_slot, own_self)
        sides = (0, 1) if p == 0 else (1,)
        n = 64 * len(sides)
        xg, part, recv, back = ((xg0, part0, recv0, back0), (xg1, part1, recv1, back1))[p]
        for k, m in enumerate(sides):
            found = nn_dot(mx[m], g[p].reshape(BLOCK, W))
            for d in range(NY):
                rows = found[:, 128 * d : 128 * d + 128]
                step = n // 8
                part[d, pl.ds(64 // step * k, 64 // step)] = rows.reshape(
                    64 // step, step, 128
                ).astype(part.dtype)
        out_slot, back_slot = links.slot(), links.slot()

        def to_all(copy_of):
            def start(e, _):
                copy_of(e).start()
                return 0

            lax.fori_loop(1, 32, start, 0)

        def piece(e):
            peer_y, peer_z = yz_peer(e)
            return links.make(
                part.at[peer_y, peer_z], recv.at[e - 1], at(yy=peer_y, zz=peer_z), out_slot
            )

        to_all(piece)
        every = links.make(recv, recv, mate, out_slot)
        links.pending.append((every, None))
        yield
        every.wait_recv()
        total_yz = part[y, z].astype(F32)
        for e in range(1, 32):
            total_yz = total_yz + recv[e - 1].astype(F32)
        back[y, z] = total_yz.astype(back.dtype)

        def reply(e):
            peer_y, peer_z = yz_peer(e)
            return links.make(
                back.at[y, z], back.at[y, z], at(yy=peer_y, zz=peer_z), back_slot
            )

        to_all(reply)
        every = links.make(recv, recv, mate, back_slot)
        links.pending.append((every, None))
        yield
        every.wait_recv()
        xg[j] = back[...].reshape(NY, n, 128).astype(BF16)
        yield from over_x_core(lambda k: xg.at[k], lambda k, h: xg.at[k, pl.ds(2 * h, 2)])
        yield

    parts = {
        "f": panel_gather(0),
        "s": panel_gather(1),
        "A": chain(0),
        "B": chain(1),
    }
    for name in ORDER:
        if name == "m":
            links.arrived(ax, mate, a_slot)
            mask_rows(ax, c + 1 - 2 * core)
        elif name == "o":
            send_own_rows()
        else:
            next(parts[name])
    links.drain()


ORDER = "mffsffsfsf" + "AsAAsAsA" + "BBBA" + "BoABAAB" + "AABBABBABABABABBB"
N_COPIES = 128


def finish(
        inner_ref,
    pivot1_ref,
    pivot2_ref,
    xg0,
    xg1,
    c1_ref,
    c2_ref,
    d1_out,
    i2_out,
    d2_out,
    c1_out,
    c2_out,
    d1,
    i2,
    d2,
    crossed,
    sem,
):
    def assemble(out, source, first, pivot):
        for k in range(8):
            for d in range(NY):
                rows, cols = slice(64 * k, 64 * k + 64), slice(128 * d, 128 * d + 128)
                part = source[k, d, first : first + 64].astype(F32)
                out[rows, cols] = part if pivot is None else pivot[rows, cols] - part

    def parts_dot(dot, wide):
        high = wide.astype(BF16)
        low = (wide - high.astype(F32)).astype(BF16)
        return dot(high) + dot(low)

    copies = [
        pltpu.make_async_copy(c1_ref, c1_out, sem.at[3]),
        pltpu.make_async_copy(c2_ref, c2_out, sem.at[4]),
        pltpu.make_async_copy(d1, d1_out, sem.at[0]),
        pltpu.make_async_copy(i2, i2_out, sem.at[1]),
        pltpu.make_async_copy(d2, d2_out, sem.at[2]),
    ]
    copies[0].start()
    copies[1].start()
    inner = inner_ref[...]
    assemble(d1, xg0, 0, pivot1_ref)
    copies[2].start()
    assemble(crossed, xg0, 64, None)
    i2[...] = -(parts_dot(lambda v: nn_dot(v, inner), d1[...]) + crossed[...].T)
    copies[3].start()
    inner_t = inner.T
    assemble(d2, xg1, 0, pivot2_ref)
    d2[...] = d2[...] - parts_dot(lambda v: nn_dot(inner_t, v), i2[...])
    copies[4].start()
    for copy in copies:
        copy.wait()


def body(
    ancestor_inverse,
    tile_pattern,
    rows_first,
    rows_second,
    panel_first,
    panel_second,
    inner_panel,
    pivot_first,
    pivot_second,
):
    col_block = ancestor_inverse.shape[1]
    halves = ancestor_inverse.reshape(NZH, NX, NC, SHARE, col_block)
    anywhere = pl.BlockSpec(memory_space=pl.ANY)
    in_hbm = pl.BlockSpec(memory_space=pltpu.HBM)
    vmem = pl.BlockSpec(memory_space=pltpu.VMEM)
    wide = jax.ShapeDtypeStruct((W, W), F32)
    column_first, column_second, gathered0, gathered1 = pl.pallas_call(
        kernel,
        out_shape=(
            jax.ShapeDtypeStruct((SHARE, W), BF16),
            jax.ShapeDtypeStruct((SHARE, W), BF16),
            jax.ShapeDtypeStruct((8, NY, 128, 128), BF16),
            jax.ShapeDtypeStruct((8, NY, 64, 128), BF16),
        ),
        in_specs=[in_hbm] * 7,
        out_specs=(vmem, vmem, vmem, vmem),
        scratch_shapes=[
            pltpu.VMEM((NZH, NX, SHARE, BLOCK), BF16),
            pltpu.VMEM((NZH, NX, SHARE, BLOCK), BF16),
            pltpu.SMEM((64, 64), jnp.int32),
            pltpu.VMEM((2, 16, 3072), BF16),
            pltpu.VMEM((2, 24, 128), jnp.int32),
            pltpu.VMEM((W, W), BF16),
            pltpu.VMEM((2, 16, 3072), BF16),
            pltpu.VMEM((8, 2, 64, BLOCK), BF16),
            pltpu.VMEM((8, 2, 64, BLOCK), BF16),
            pltpu.VMEM((2, 64, BLOCK), BF16),
            pltpu.VMEM((2, 3, NZH, SHARE, W), BF16),
            pltpu.VMEM((2, NZH, SHARE, W), F32),
            pltpu.VMEM((2, 2, 2, SHARE, W), BF16),
            pltpu.VMEM((2, 2, NZH, SHARE, W), BF16),
            pltpu.VMEM((2, 3, SHARE, W), BF16),
            pltpu.VMEM((2, SHARE, W), F32),
            pltpu.VMEM((2, 2, SHARE // 2, W), BF16),
            pltpu.VMEM((2, 2, SHARE, W), BF16),
            pltpu.VMEM((2, 8, SHARE, W), BF16),
            pltpu.VMEM((NY, 8, 16, 128), BF16),
            pltpu.VMEM((31, 16, 128), BF16),
            pltpu.VMEM((NY, 8, 16, 128), BF16),
            pltpu.VMEM((NY, 8, 8, 128), F32),
            pltpu.VMEM((31, 8, 128), F32),
            pltpu.VMEM((NY, 8, 8, 128), F32),
            pltpu.SemaphoreType.DMA((N_COPIES,)),
            pltpu.SemaphoreType.DMA((N_COPIES,)),
            pltpu.SemaphoreType.DMA((9,)),
        ],
        compiler_params=pltpu.CompilerParams(
            collective_id=0, has_side_effects=True, vmem_limit_bytes=48 * 2**20
        ),
    )(
        *(
            pltpu.with_memory_space_constraint(array, pltpu.HBM)
            for array in (
                halves,
                tile_pattern,
                panel_first.T,
                panel_second.T,
                rows_first.reshape(-1, 128),
                rows_second.reshape(-1, 128),
                inner_panel,
            )
        )
    )
    narrow = jax.ShapeDtypeStruct((SHARE, W), BF16)
    diagonal_first, inner_second, diagonal_second, column_first, column_second = pl.pallas_call(
        finish,
        out_shape=(wide, wide, wide, narrow, narrow),
        in_specs=[vmem] * 7,
        out_specs=(anywhere,) * 5,
        scratch_shapes=[pltpu.VMEM((W, W), F32)] * 4 + [pltpu.SemaphoreType.DMA((5,))],
        compiler_params=pltpu.CompilerParams(vmem_limit_bytes=32 * 2**20),
    )(
        inner_panel, pivot_first, pivot_second, gathered0, gathered1, column_first, column_second
    )
    return (column_first, diagonal_first, inner_second, column_second, diagonal_second)


def solution(mesh):
    return jax.shard_map(
        body,
        mesh=mesh,
        in_specs=(
            P("prow", "pcol"),
            P(),
            P(),
            P(),
            P("prow", "pcol"),
            P("prow", "pcol"),
            P(),
            P(),
            P(),
        ),
        out_specs=(P(("prow", "pcol"), None), P(), P(), P(("prow", "pcol"), None), P()),
        check_vma=False,
    )
```

```python
import jax
import jax.numpy as jnp
from jax import lax
from jax.experimental import pallas as pl
from jax.experimental.pallas import tpu as pltpu
from jax.sharding import PartitionSpec as P

TILE = 384
MESH = pl.DeviceIdType.MESH
BF16 = jnp.bfloat16
F32 = jnp.float32

NY, NX, NZH, NZL, NC = 4, 4, 4, 2, 2
BLOCK = 768
SHARE = 96
W = 512


def nt_dot(left, right):
    return lax.dot_general(left, right, (((1,), (1,)), ((), ())), preferred_element_type=F32)


def nn_dot(left, right):
    return jnp.dot(left, right, preferred_element_type=F32)


class Links:
    def __init__(self, send_sem, recv_sem):
        self.send_sem = send_sem
        self.recv_sem = recv_sem
        self.used = 0
        self.pending = []

    def slot(self):
        self.used += 1
        return self.used - 1

    def make(self, src, dst, device, slot):
        return pltpu.make_async_remote_copy(
            src_ref=src,
            dst_ref=dst,
            send_sem=self.send_sem.at[slot],
            recv_sem=self.recv_sem.at[slot],
            device_id=device,
            device_id_type=MESH,
        )

    def send(self, src, dst, device, slot=None, unless=None):
        slot = self.slot() if slot is None else slot
        copy = self.make(src, dst, device, slot)
        if unless is None:
            copy.start()
        else:
            pl.when(jnp.logical_not(unless))(copy.start)
        self.pending.append((copy, unless))
        return slot

    def arrived(self, ref, device, slot, unless=None):
        copy = self.make(ref, ref, device, slot)
        if unless is None:
            copy.wait_recv()
        else:
            pl.when(jnp.logical_not(unless))(copy.wait_recv)

    def drain(self):
        for copy, unless in self.pending:
            if unless is None:
                copy.wait_send()
            else:
                pl.when(jnp.logical_not(unless))(copy.wait_send)
        self.pending = []


def kernel(
    a_ref,
    pattern_ref,
    panel1_ref,
    panel2_ref,
    rows1_ref,
    rows2_ref,
    inner_ref,
    c1_ref,
    c2_ref,
    xg0,
    xg1,
    ao,
    ax,
    pattern,
    panels,
    rows,
    inner,
    xt,
    pt,
    ptx,
    mx,
    t,
    town,
    rxd,
    rx,
    s1,
    s1own,
    rzd,
    rz,
    g,
    part0,
    recv0,
    back0,
    part1,
    recv1,
    back1,
    send_sem,
    recv_sem,
    local_sem,
):
    r = lax.axis_index("prow")
    c = lax.axis_index("pcol")
    y = r % NY
    zl = r // NY
    zh = c // 8
    x = (c // 2) % NX
    core = c % 2
    j = c % 8
    z = zh * 2 + zl

    def at(yy=None, zz=None, xx=None, cc=None):
        yy = y if yy is None else yy
        zz = z if zz is None else zz
        xx = x if xx is None else xx
        cc = core if cc is None else cc
        return ((zz % 2) * NY + yy, (zz // 2) * 8 + xx * 2 + cc)

    mate = at(cc=1 - core)
    xn, xp = at(xx=(x + 1) % NX), at(xx=(x + 3) % NX)
    zhn, zhp = at(zz=(z + 2) % 8), at(zz=(z + 6) % 8)
    yn, yp = at(yy=(y + 1) % NY), at(yy=(y + 3) % NY)
    zmate = at(zz=zh * 2 + 1 - zl)
    def yz_peer(e):
        return (y + e // 8) % NY, (z + e % 8) % 8

    barrier = pltpu.get_barrier_semaphore()
    first_self = c // 4 == r
    own_self = (c // 4 == r) & (8 * (c % 4) + r == c)
    for device in [mate, xn, xp]:
        pl.semaphore_signal(barrier, inc=1, device_id=device, device_id_type=MESH)

    def greet(e, _):
        peer_y, peer_z = yz_peer(e)
        pl.semaphore_signal(
            barrier, inc=1, device_id=at(yy=peer_y, zz=peer_z), device_id_type=MESH
        )
        return 0

    lax.fori_loop(1, 32, greet, 0)
    for i in range(4):

        @pl.when(jnp.logical_not(first_self & (c % 4 == i)))
        def _():
            pl.semaphore_signal(barrier, inc=1, device_id=(c // 4, 4 * r + i), device_id_type=MESH)

    @pl.when(jnp.logical_not(own_self))
    def _():
        pl.semaphore_signal(barrier, inc=1, device_id=(j, 4 * r + zh), device_id_type=MESH)

    own_rows = pl.ds(pl.multiple_of(24 * r, 8), 24)
    loads = [
        pltpu.make_async_copy(rows1_ref.at[own_rows], rows.at[0], local_sem.at[3]),
        pltpu.make_async_copy(rows2_ref.at[own_rows], rows.at[1], local_sem.at[4]),
        pltpu.make_async_copy(panel1_ref, panels.at[0], local_sem.at[5]),
        pltpu.make_async_copy(panel2_ref, panels.at[1], local_sem.at[6]),
        pltpu.make_async_copy(pattern_ref, pattern, local_sem.at[7]),
        pltpu.make_async_copy(a_ref.at[:, :, core], ao, local_sem.at[0]),
        pltpu.make_async_copy(inner_ref, inner, local_sem.at[8]),
    ]
    for load in loads:
        load.start()
    for load in loads[:4]:
        load.wait()
    keep1 = rows[0].astype(F32)
    keep2 = keep1 * rows[1].astype(F32)
    for p, keep in enumerate((keep1, keep2)):
        for k in range(24):
            cut = slice(128 * k, 128 * k + 128)
            xt[p, :, cut] = (panels[p, :, cut].astype(F32) * keep[k : k + 1]).astype(BF16)

    pl.semaphore_wait(
        barrier, 34 + 5 - first_self.astype(jnp.int32) - own_self.astype(jnp.int32)
    )

    links = Links(send_sem, recv_sem)

    slice16 = pl.ds(pl.multiple_of(16 * (c % 4), 16), 16)
    base_first = [links.slot() for _ in range(8)][0]
    own_slot = links.slot()

    def spread(source, target, base, device, me, q, spare):
        copy = pltpu.make_async_remote_copy(
            src_ref=source,
            dst_ref=target,
            send_sem=send_sem.at[base + q],
            recv_sem=recv_sem.at[base + c % 4],
            device_id=device,
            device_id_type=MESH,
        )
        pl.when(jnp.logical_not(me))(copy.start)
        links.pending.append((copy, me))

        @pl.when(me)
        def _():
            local = pltpu.make_async_copy(source, target, local_sem.at[spare])
            local.start()
            local.wait()

    def spread_panel(p):
        for q in range(4):
            spread(
                xt.at[p, :, pl.ds(768 * q, 768)],
                pt.at[c // 4, p, slice16, :],
                base_first + 4 * p,
                (c // 4, 4 * r + q),
                first_self & (c % 4 == q),
                q,
                1,
            )

    spread_panel(0)

    a_slot = links.send(a_ref.at[:, :, 1 - core], ax, mate)

    def send_own_rows():
        links.send(pt.at[r], mx, (c // 4, 8 * (c % 4) + r), own_slot, own_self)

        @pl.when(own_self)
        def _():
            local = pltpu.make_async_copy(pt.at[r], mx, local_sem.at[2])
            local.start()
            local.wait()

    def mask_rows(ref, owner):
        def chunk(i, _):
            m = i // NX
            n = i % NX
            for k in range(2):
                cut = slice(TILE * k, TILE * k + TILE)
                keep = pattern[8 * r + 2 * m + n // 2, 2 * owner + k].astype(F32)
                ref[m, n, :, cut] = (ref[m, n, :, cut].astype(F32) * keep).astype(BF16)
            return 0

        lax.fori_loop(0, NZH * NX, chunk, 0)

    for load in loads[4:]:
        load.wait()
    mask_rows(ao, c)

    def row_of(yy, zz):
        return zz * NY + yy

    r_z = row_of(y, 1 - zl)
    y_p, y_n, y_d = (y + 3) % NY, (y + 1) % NY, (y + 2) % NY

    def panel_gather(p):
        forwarded = []

        def to(device, row):
            return links.send(pt.at[row, p], pt.at[row, p], device)

        def to_mate(row):
            forwarded.append((row, links.send(pt.at[row, p], ptx.at[row, p], mate)))

        def part(row, h):
            return pt.at[row, p, pl.ds(32 * h, 32)]

        for i in range(4):
            links.arrived(
                pt.at[r, p, pl.ds(16 * i, 16), :],
                mate,
                base_first + 4 * p + i,
                first_self & (c % 4 == i),
            )
        got_z, got_yp, got_yn = to(zmate, r), to(yn, r), to(yp, r)
        to_mate(r)
        yield
        links.arrived(pt.at[r_z, p], zmate, got_z)
        got_yp_z, got_yn_z = to(yn, r_z), to(yp, r_z)
        to_mate(r_z)
        yield
        relayed = []
        for zz, slot_p, slot_n in ((zl, got_yp, got_yn), (1 - zl, got_yp_z, got_yn_z)):
            row_p, row_n, row_d = row_of(y_p, zz), row_of(y_n, zz), row_of(y_d, zz)
            links.arrived(pt.at[row_p, p], yp, slot_p)
            got_d0 = links.send(part(row_p, 0), part(row_p, 0), yn)
            links.arrived(pt.at[row_n, p], yn, slot_n)
            got_d1 = links.send(part(row_n, 1), part(row_n, 1), yp)
            to_mate(row_p)
            to_mate(row_n)
            relayed.append((row_d, got_d0, got_d1))
            yield
        for row_d, got_d0, got_d1 in relayed:
            links.arrived(part(row_d, 0), yp, got_d0)
            links.arrived(part(row_d, 1), yn, got_d1)
            to_mate(row_d)
        yield
        for row, slot in forwarded:
            links.arrived(ptx.at[row, p], mate, slot)
        yield

    def product(p, xx, out):
        left = ao[:, xx].reshape(NZH * SHARE, BLOCK)
        left_x = ax[:, xx].reshape(NZH * SHARE, BLOCK)
        for h in range(2):
            right = pt[pl.ds(4 * h, 4), p].reshape(256, BLOCK)
            right_x = ptx[pl.ds(4 * h, 4), p].reshape(256, BLOCK)
            value = nt_dot(left, right) + nt_dot(left_x, right_x)
            out[..., pl.ds(256 * h, 256)] = value.reshape(NZH, SHARE, 256).astype(out.dtype)

    half = SHARE // 2
    lo, hi = pl.ds(0, half), pl.ds(half, half)
    zh_n, zh_p, zh_d = (zh + 1) % NZH, (zh + 3) % NZH, (zh + 2) % NZH
    jn, jp, jd = (j + 2) % 8, (j + 6) % 8, (j + 4) % 8

    def over_x_core(buf, part):
        own_p = links.send(buf(j), buf(j), xn)
        own_n = links.send(buf(j), buf(j), xp)
        own_m = links.send(buf(j), buf(j), mate)
        yield
        links.arrived(buf(jp), xp, own_p)
        d0 = links.send(part(jp, 0), part(jp, 0), xn)
        links.arrived(buf(jn), xn, own_n)
        d1 = links.send(part(jn, 1), part(jn, 1), xp)
        m_p = links.send(buf(jp), buf(jp), mate)
        m_n = links.send(buf(jn), buf(jn), mate)
        yield
        links.arrived(part(jd, 0), xp, d0)
        links.arrived(part(jd, 1), xn, d1)
        m_d = links.send(buf(jd), buf(jd), mate)
        yield
        other = 1 - 2 * core
        links.arrived(buf(j + other), mate, own_m)
        links.arrived(buf(jp + other), mate, m_p)
        links.arrived(buf(jn + other), mate, m_n)
        links.arrived(buf(jd + other), mate, m_d)

    def chain(p):
        product(p, (x + 2) % NX, t.at[p, 0])
        got_p = links.send(t.at[p, 0, pl.ds(0, 2)], rxd.at[p, 0], xn)
        got_n = links.send(t.at[p, 0, pl.ds(2, 2)], rxd.at[p, 1], xp)
        yield
        product(p, (x + 1) % NX, t.at[p, 1])
        pure_p = links.send(t.at[p, 1, pl.ds(2, 2)], rx.at[p, 0, pl.ds(2, 2)], xn)
        yield
        product(p, (x + 3) % NX, t.at[p, 2])
        pure_n = links.send(t.at[p, 2, pl.ds(0, 2)], rx.at[p, 1, pl.ds(0, 2)], xp)
        yield
        links.arrived(rxd.at[p, 0], xp, got_p)
        t[p, 1, 0:2] = (t[p, 1, 0:2].astype(F32) + rxd[p, 0].astype(F32)).astype(BF16)
        sum_p = links.send(t.at[p, 1, pl.ds(0, 2)], rx.at[p, 0, pl.ds(0, 2)], xn)
        links.arrived(rxd.at[p, 1], xn, got_n)
        t[p, 2, 2:4] = (t[p, 2, 2:4].astype(F32) + rxd[p, 1].astype(F32)).astype(BF16)
        sum_n = links.send(t.at[p, 2, pl.ds(2, 2)], rx.at[p, 1, pl.ds(2, 2)], xp)
        yield
        product(p, x, town.at[p])
        yield
        links.arrived(rx.at[p, 0, pl.ds(2, 2)], xp, pure_p)
        links.arrived(rx.at[p, 1, pl.ds(0, 2)], xn, pure_n)
        links.arrived(rx.at[p, 0, pl.ds(0, 2)], xp, sum_p)
        links.arrived(rx.at[p, 1, pl.ds(2, 2)], xn, sum_n)

        def total(k):
            return town[p, k] + rx[p, 0, k].astype(F32) + rx[p, 1, k].astype(F32)

        s1[p, 0] = total(zh_d).astype(BF16)
        got_p = links.send(s1.at[p, 0, lo], rzd.at[p, 0], zhn)
        got_n = links.send(s1.at[p, 0, hi], rzd.at[p, 1], zhp)
        s1[p, 1] = total(zh_n).astype(BF16)
        pure_p = links.send(s1.at[p, 1, hi], rz.at[p, 0, hi], zhn)
        s1[p, 2] = total(zh_p).astype(BF16)
        pure_n = links.send(s1.at[p, 2, lo], rz.at[p, 1, lo], zhp)
        s1own[p] = total(zh)
        yield
        links.arrived(rzd.at[p, 0], zhp, got_p)
        s1[p, 1, lo] = (s1[p, 1, lo].astype(F32) + rzd[p, 0].astype(F32)).astype(BF16)
        sum_p = links.send(s1.at[p, 1, lo], rz.at[p, 0, lo], zhn)
        links.arrived(rzd.at[p, 1], zhn, got_n)
        s1[p, 2, hi] = (s1[p, 2, hi].astype(F32) + rzd[p, 1].astype(F32)).astype(BF16)
        sum_n = links.send(s1.at[p, 2, hi], rz.at[p, 1, hi], zhp)
        yield
        links.arrived(rz.at[p, 0, hi], zhp, pure_p)
        links.arrived(rz.at[p, 1, lo], zhn, pure_n)
        links.arrived(rz.at[p, 0, lo], zhp, sum_p)
        links.arrived(rz.at[p, 1, hi], zhn, sum_n)
        total_sum = s1own[p] + rz[p, 0].astype(F32) + rz[p, 1].astype(F32)
        if p == 0:
            column = (-total_sum).astype(BF16)
            c1_ref[...] = column
        else:
            column = (-(total_sum + nn_dot(c1_ref[...], inner[...]))).astype(BF16)
            c2_ref[...] = column
        g[p, j] = column
        yield from over_x_core(
            lambda k: g.at[p, k], lambda k, h: g.at[p, k, pl.ds(half * h, half)]
        )

        if p == 0:
            links.arrived(mx, mate, own_slot, own_self)
        sides = (0, 1) if p == 0 else (1,)
        n = 64 * len(sides)
        xg, part, recv, back = ((xg0, part0, recv0, back0), (xg1, part1, recv1, back1))[p]
        for k, m in enumerate(sides):
            found = nn_dot(mx[m], g[p].reshape(BLOCK, W))
            for d in range(NY):
                rows = found[:, 128 * d : 128 * d + 128]
                step = n // 8
                part[d, pl.ds(64 // step * k, 64 // step)] = rows.reshape(
                    64 // step, step, 128
                ).astype(part.dtype)
        out_slot, back_slot = links.slot(), links.slot()

        def to_all(copy_of):
            def start(e, _):
                copy_of(e).start()
                return 0

            lax.fori_loop(1, 32, start, 0)

        def piece(e):
            peer_y, peer_z = yz_peer(e)
            return links.make(
                part.at[peer_y, peer_z], recv.at[e - 1], at(yy=peer_y, zz=peer_z), out_slot
            )

        to_all(piece)
        every = links.make(recv, recv, mate, out_slot)
        links.pending.append((every, None))
        yield
        every.wait_recv()
        total_yz = part[y, z].astype(F32)
        for e in range(1, 32):
            total_yz = total_yz + recv[e - 1].astype(F32)
        back[y, z] = total_yz.astype(back.dtype)

        def reply(e):
            peer_y, peer_z = yz_peer(e)
            return links.make(
                back.at[y, z], back.at[y, z], at(yy=peer_y, zz=peer_z), back_slot
            )

        to_all(reply)
        every = links.make(recv, recv, mate, back_slot)
        links.pending.append((every, None))
        yield
        every.wait_recv()
        xg[j] = back[...].reshape(NY, n, 128).astype(BF16)
        yield from over_x_core(lambda k: xg.at[k], lambda k, h: xg.at[k, pl.ds(2 * h, 2)])
        yield

    parts = {
        "f": panel_gather(0),
        "s": panel_gather(1),
        "A": chain(0),
        "B": chain(1),
    }
    for name in ORDER:
        if name == "m":
            links.arrived(ax, mate, a_slot)
            mask_rows(ax, c + 1 - 2 * core)
        elif name == "o":
            send_own_rows()
        elif name == "t":
            spread_panel(1)
        else:
            next(parts[name])
    links.drain()


ORDER = "mftffsofsffAsAAsAsAsBBBABABAABAABBBABBABABABABB"
N_COPIES = 128


def finish(
        inner_ref,
    pivot1_ref,
    pivot2_ref,
    xg0,
    xg1,
    c1_ref,
    c2_ref,
    d1_out,
    i2_out,
    d2_out,
    c1_out,
    c2_out,
    d1,
    i2,
    d2,
    crossed,
    sem,
):
    def assemble(out, source, first, pivot):
        for k in range(8):
            for d in range(NY):
                rows, cols = slice(64 * k, 64 * k + 64), slice(128 * d, 128 * d + 128)
                part = source[k, d, first : first + 64].astype(F32)
                out[rows, cols] = part if pivot is None else pivot[rows, cols] - part

    def parts_dot(dot, wide):
        high = wide.astype(BF16)
        low = (wide - high.astype(F32)).astype(BF16)
        return dot(high) + dot(low)

    copies = [
        pltpu.make_async_copy(c1_ref, c1_out, sem.at[3]),
        pltpu.make_async_copy(c2_ref, c2_out, sem.at[4]),
        pltpu.make_async_copy(d1, d1_out, sem.at[0]),
        pltpu.make_async_copy(i2, i2_out, sem.at[1]),
        pltpu.make_async_copy(d2, d2_out, sem.at[2]),
    ]
    copies[0].start()
    copies[1].start()
    inner = inner_ref[...]
    assemble(d1, xg0, 0, pivot1_ref)
    copies[2].start()
    assemble(crossed, xg0, 64, None)
    i2[...] = -(parts_dot(lambda v: nn_dot(v, inner), d1[...]) + crossed[...].T)
    copies[3].start()
    inner_t = inner.T
    assemble(d2, xg1, 0, pivot2_ref)
    d2[...] = d2[...] - parts_dot(lambda v: nn_dot(inner_t, v), i2[...])
    copies[4].start()
    for copy in copies:
        copy.wait()


def body(
    ancestor_inverse,
    tile_pattern,
    rows_first,
    rows_second,
    panel_first,
    panel_second,
    inner_panel,
    pivot_first,
    pivot_second,
):
    col_block = ancestor_inverse.shape[1]
    halves = ancestor_inverse.reshape(NZH, NX, NC, SHARE, col_block)
    anywhere = pl.BlockSpec(memory_space=pl.ANY)
    in_hbm = pl.BlockSpec(memory_space=pltpu.HBM)
    vmem = pl.BlockSpec(memory_space=pltpu.VMEM)
    wide = jax.ShapeDtypeStruct((W, W), F32)
    column_first, column_second, gathered0, gathered1 = pl.pallas_call(
        kernel,
        out_shape=(
            jax.ShapeDtypeStruct((SHARE, W), BF16),
            jax.ShapeDtypeStruct((SHARE, W), BF16),
            jax.ShapeDtypeStruct((8, NY, 128, 128), BF16),
            jax.ShapeDtypeStruct((8, NY, 64, 128), BF16),
        ),
        in_specs=[in_hbm] * 7,
        out_specs=(vmem, vmem, vmem, vmem),
        scratch_shapes=[
            pltpu.VMEM((NZH, NX, SHARE, BLOCK), BF16),
            pltpu.VMEM((NZH, NX, SHARE, BLOCK), BF16),
            pltpu.SMEM((64, 64), jnp.int32),
            pltpu.VMEM((2, 16, 3072), BF16),
            pltpu.VMEM((2, 24, 128), jnp.int32),
            pltpu.VMEM((W, W), BF16),
            pltpu.VMEM((2, 16, 3072), BF16),
            pltpu.VMEM((8, 2, 64, BLOCK), BF16),
            pltpu.VMEM((8, 2, 64, BLOCK), BF16),
            pltpu.VMEM((2, 64, BLOCK), BF16),
            pltpu.VMEM((2, 3, NZH, SHARE, W), BF16),
            pltpu.VMEM((2, NZH, SHARE, W), F32),
            pltpu.VMEM((2, 2, 2, SHARE, W), BF16),
            pltpu.VMEM((2, 2, NZH, SHARE, W), BF16),
            pltpu.VMEM((2, 3, SHARE, W), BF16),
            pltpu.VMEM((2, SHARE, W), F32),
            pltpu.VMEM((2, 2, SHARE // 2, W), BF16),
            pltpu.VMEM((2, 2, SHARE, W), BF16),
            pltpu.VMEM((2, 8, SHARE, W), BF16),
            pltpu.VMEM((NY, 8, 16, 128), BF16),
            pltpu.VMEM((31, 16, 128), BF16),
            pltpu.VMEM((NY, 8, 16, 128), BF16),
            pltpu.VMEM((NY, 8, 8, 128), F32),
            pltpu.VMEM((31, 8, 128), F32),
            pltpu.VMEM((NY, 8, 8, 128), F32),
            pltpu.SemaphoreType.DMA((N_COPIES,)),
            pltpu.SemaphoreType.DMA((N_COPIES,)),
            pltpu.SemaphoreType.DMA((9,)),
        ],
        compiler_params=pltpu.CompilerParams(
            collective_id=0, has_side_effects=True, vmem_limit_bytes=48 * 2**20
        ),
    )(
        *(
            pltpu.with_memory_space_constraint(array, pltpu.HBM)
            for array in (
                halves,
                tile_pattern,
                panel_first.T,
                panel_second.T,
                rows_first.reshape(-1, 128),
                rows_second.reshape(-1, 128),
                inner_panel,
            )
        )
    )
    narrow = jax.ShapeDtypeStruct((SHARE, W), BF16)
    diagonal_first, inner_second, diagonal_second, column_first, column_second = pl.pallas_call(
        finish,
        out_shape=(wide, wide, wide, narrow, narrow),
        in_specs=[vmem] * 7,
        out_specs=(anywhere,) * 5,
        scratch_shapes=[pltpu.VMEM((W, W), F32)] * 4 + [pltpu.SemaphoreType.DMA((5,))],
        compiler_params=pltpu.CompilerParams(vmem_limit_bytes=32 * 2**20),
    )(
        inner_panel, pivot_first, pivot_second, gathered0, gathered1, column_first, column_second
    )
    return (column_first, diagonal_first, inner_second, column_second, diagonal_second)


def solution(mesh):
    return jax.shard_map(
        body,
        mesh=mesh,
        in_specs=(
            P("prow", "pcol"),
            P(),
            P(),
            P(),
            P("prow", "pcol"),
            P("prow", "pcol"),
            P(),
            P(),
            P(),
        ),
        out_specs=(P(("prow", "pcol"), None), P(), P(), P(("prow", "pcol"), None), P()),
        check_vma=False,
    )
```

```python
import jax
import jax.numpy as jnp
from jax import lax
from jax.experimental import pallas as pl
from jax.experimental.pallas import tpu as pltpu
from jax.sharding import PartitionSpec as P

TILE = 384
MESH = pl.DeviceIdType.MESH
BF16 = jnp.bfloat16
F32 = jnp.float32

NY, NX, NZH, NZL, NC = 4, 4, 4, 2, 2
BLOCK = 768
SHARE = 96
W = 512


def nt_dot(left, right):
    return lax.dot_general(left, right, (((1,), (1,)), ((), ())), preferred_element_type=F32)


def nn_dot(left, right):
    return jnp.dot(left, right, preferred_element_type=F32)


class Links:
    def __init__(self, send_sem, recv_sem):
        self.send_sem = send_sem
        self.recv_sem = recv_sem
        self.used = 0
        self.pending = []

    def slot(self):
        self.used += 1
        return self.used - 1

    def make(self, src, dst, device, slot):
        return pltpu.make_async_remote_copy(
            src_ref=src,
            dst_ref=dst,
            send_sem=self.send_sem.at[slot],
            recv_sem=self.recv_sem.at[slot],
            device_id=device,
            device_id_type=MESH,
        )

    def send(self, src, dst, device, slot=None, unless=None):
        slot = self.slot() if slot is None else slot
        copy = self.make(src, dst, device, slot)
        if unless is None:
            copy.start()
        else:
            pl.when(jnp.logical_not(unless))(copy.start)
        self.pending.append((copy, unless))
        return slot

    def arrived(self, ref, device, slot, unless=None):
        copy = self.make(ref, ref, device, slot)
        if unless is None:
            copy.wait_recv()
        else:
            pl.when(jnp.logical_not(unless))(copy.wait_recv)

    def drain(self):
        for copy, unless in self.pending:
            if unless is None:
                copy.wait_send()
            else:
                pl.when(jnp.logical_not(unless))(copy.wait_send)
        self.pending = []


def kernel(
    a_ref,
    pattern_ref,
    panel1_ref,
    panel2_ref,
    rows1_ref,
    rows2_ref,
    inner_ref,
    c1_ref,
    c2_ref,
    xg0,
    xg1,
    ao,
    ax,
    pattern,
    panels,
    rows,
    inner,
    xt,
    pt,
    ptx,
    mx,
    t,
    town,
    rxd,
    rx,
    s1,
    s1own,
    rzd,
    rz,
    g,
    part0,
    recv0,
    back0,
    part1,
    recv1,
    back1,
    send_sem,
    recv_sem,
    local_sem,
):
    r = lax.axis_index("prow")
    c = lax.axis_index("pcol")
    y = r % NY
    zl = r // NY
    zh = c // 8
    x = (c // 2) % NX
    core = c % 2
    j = c % 8
    z = zh * 2 + zl

    def at(yy=None, zz=None, xx=None, cc=None):
        yy = y if yy is None else yy
        zz = z if zz is None else zz
        xx = x if xx is None else xx
        cc = core if cc is None else cc
        return ((zz % 2) * NY + yy, (zz // 2) * 8 + xx * 2 + cc)

    mate = at(cc=1 - core)
    xn, xp = at(xx=(x + 1) % NX), at(xx=(x + 3) % NX)
    zhn, zhp = at(zz=(z + 2) % 8), at(zz=(z + 6) % 8)
    yn, yp = at(yy=(y + 1) % NY), at(yy=(y + 3) % NY)
    zmate = at(zz=zh * 2 + 1 - zl)
    def yz_peer(e):
        return (y + e // 8) % NY, (z + e % 8) % 8

    barrier = pltpu.get_barrier_semaphore()
    first_self = (c // 4 == r) & (j == r)
    own_self = (c // 4 == r) & (8 * (c % 4) + r == c)
    for device in [mate, xn, xp]:
        pl.semaphore_signal(barrier, inc=1, device_id=device, device_id_type=MESH)

    def greet(e, _):
        peer_y, peer_z = yz_peer(e)
        pl.semaphore_signal(
            barrier, inc=1, device_id=at(yy=peer_y, zz=peer_z), device_id_type=MESH
        )
        return 0

    lax.fori_loop(1, 32, greet, 0)
    for i in range(4):

        @pl.when(jnp.logical_not(first_self & (zh == i)))
        def _():
            pl.semaphore_signal(barrier, inc=1, device_id=(c // 4, 8 * i + r), device_id_type=MESH)

    @pl.when(jnp.logical_not(own_self))
    def _():
        pl.semaphore_signal(barrier, inc=1, device_id=(j, 4 * r + zh), device_id_type=MESH)

    own_rows = pl.ds(pl.multiple_of(24 * r, 8), 24)
    loads = [
        pltpu.make_async_copy(rows1_ref.at[own_rows], rows.at[0], local_sem.at[3]),
        pltpu.make_async_copy(rows2_ref.at[own_rows], rows.at[1], local_sem.at[4]),
        pltpu.make_async_copy(panel1_ref, panels.at[0], local_sem.at[5]),
        pltpu.make_async_copy(panel2_ref, panels.at[1], local_sem.at[6]),
        pltpu.make_async_copy(pattern_ref, pattern, local_sem.at[7]),
        pltpu.make_async_copy(a_ref.at[:, :, core], ao, local_sem.at[0]),
        pltpu.make_async_copy(inner_ref, inner, local_sem.at[8]),
    ]
    for load in loads:
        load.start()
    for load in loads[:4]:
        load.wait()
    keep1 = rows[0].astype(F32)
    keep2 = keep1 * rows[1].astype(F32)
    for p, keep in enumerate((keep1, keep2)):
        for k in range(24):
            cut = slice(128 * k, 128 * k + 128)
            xt[p, :, cut] = (panels[p, :, cut].astype(F32) * keep[k : k + 1]).astype(BF16)

    pl.semaphore_wait(
        barrier, 34 + 5 - first_self.astype(jnp.int32) - own_self.astype(jnp.int32)
    )

    links = Links(send_sem, recv_sem)

    slice16 = pl.ds(pl.multiple_of(16 * zh, 16), 16)
    base_first = [links.slot() for _ in range(8)][0]
    own_slot = links.slot()

    def spread(source, target, base, device, me, q, spare):
        copy = pltpu.make_async_remote_copy(
            src_ref=source,
            dst_ref=target,
            send_sem=send_sem.at[base + q],
            recv_sem=recv_sem.at[base + zh],
            device_id=device,
            device_id_type=MESH,
        )
        pl.when(jnp.logical_not(me))(copy.start)
        links.pending.append((copy, me))

        @pl.when(me)
        def _():
            local = pltpu.make_async_copy(source, target, local_sem.at[spare])
            local.start()
            local.wait()

    def spread_panel(p):
        for q in range(4):
            spread(
                xt.at[p, :, pl.ds(768 * q, 768)],
                pt.at[j, p, slice16, :],
                base_first + 4 * p,
                (j, 4 * r + q),
                first_self & (c % 4 == q),
                q,
                1,
            )

    spread_panel(0)

    a_slot = links.send(a_ref.at[:, :, 1 - core], ax, mate)

    def send_own_rows():
        links.send(pt.at[r], mx, (c // 4, 8 * (c % 4) + r), own_slot, own_self)

        @pl.when(own_self)
        def _():
            local = pltpu.make_async_copy(pt.at[r], mx, local_sem.at[2])
            local.start()
            local.wait()

    def mask_rows(ref, owner):
        def chunk(i, _):
            m = i // NX
            n = i % NX
            for k in range(2):
                cut = slice(TILE * k, TILE * k + TILE)
                keep = pattern[8 * r + 2 * m + n // 2, 2 * owner + k].astype(F32)
                ref[m, n, :, cut] = (ref[m, n, :, cut].astype(F32) * keep).astype(BF16)
            return 0

        lax.fori_loop(0, NZH * NX, chunk, 0)

    for load in loads[4:]:
        load.wait()
    mask_rows(ao, c)

    def row_of(yy, zz):
        return zz * NY + yy

    r_z = row_of(y, 1 - zl)
    y_p, y_n, y_d = (y + 3) % NY, (y + 1) % NY, (y + 2) % NY

    def panel_gather(p):
        forwarded = []

        def to(device, row):
            return links.send(pt.at[row, p], pt.at[row, p], device)

        def to_mate(row):
            forwarded.append((row, links.send(pt.at[row, p], ptx.at[row, p], mate)))

        def part(row, h):
            return pt.at[row, p, pl.ds(32 * h, 32)]

        for i in range(4):
            links.arrived(
                pt.at[r, p, pl.ds(16 * i, 16), :],
                mate,
                base_first + 4 * p + i,
                first_self & (zh == i),
            )
        got_z, got_yp, got_yn = to(zmate, r), to(yn, r), to(yp, r)
        to_mate(r)
        yield
        links.arrived(pt.at[r_z, p], zmate, got_z)
        got_yp_z, got_yn_z = to(yn, r_z), to(yp, r_z)
        to_mate(r_z)
        yield
        relayed = []
        for zz, slot_p, slot_n in ((zl, got_yp, got_yn), (1 - zl, got_yp_z, got_yn_z)):
            row_p, row_n, row_d = row_of(y_p, zz), row_of(y_n, zz), row_of(y_d, zz)
            links.arrived(pt.at[row_p, p], yp, slot_p)
            got_d0 = links.send(part(row_p, 0), part(row_p, 0), yn)
            links.arrived(pt.at[row_n, p], yn, slot_n)
            got_d1 = links.send(part(row_n, 1), part(row_n, 1), yp)
            to_mate(row_p)
            to_mate(row_n)
            relayed.append((row_d, got_d0, got_d1))
            yield
        for row_d, got_d0, got_d1 in relayed:
            links.arrived(part(row_d, 0), yp, got_d0)
            links.arrived(part(row_d, 1), yn, got_d1)
            to_mate(row_d)
        yield
        for row, slot in forwarded:
            links.arrived(ptx.at[row, p], mate, slot)
        yield

    def in_order(ref, p, h):
        return jnp.concatenate(
            [ref[k, p, pl.ds(16 * i, 16)] for i in (2 * h, 2 * h + 1) for k in range(8)], axis=0
        )

    def product(p, xx, out):
        left = ao[:, xx].reshape(NZH * SHARE, BLOCK)
        left_x = ax[:, xx].reshape(NZH * SHARE, BLOCK)
        for h in range(2):
            right, right_x = in_order(pt, p, h), in_order(ptx, p, h)
            value = nt_dot(left, right) + nt_dot(left_x, right_x)
            out[..., pl.ds(256 * h, 256)] = value.reshape(NZH, SHARE, 256).astype(out.dtype)

    half = SHARE // 2
    lo, hi = pl.ds(0, half), pl.ds(half, half)
    zh_n, zh_p, zh_d = (zh + 1) % NZH, (zh + 3) % NZH, (zh + 2) % NZH
    jn, jp, jd = (j + 2) % 8, (j + 6) % 8, (j + 4) % 8

    def over_x_core(buf, part):
        own_p = links.send(buf(j), buf(j), xn)
        own_n = links.send(buf(j), buf(j), xp)
        own_m = links.send(buf(j), buf(j), mate)
        yield
        links.arrived(buf(jp), xp, own_p)
        d0 = links.send(part(jp, 0), part(jp, 0), xn)
        links.arrived(buf(jn), xn, own_n)
        d1 = links.send(part(jn, 1), part(jn, 1), xp)
        m_p = links.send(buf(jp), buf(jp), mate)
        m_n = links.send(buf(jn), buf(jn), mate)
        yield
        links.arrived(part(jd, 0), xp, d0)
        links.arrived(part(jd, 1), xn, d1)
        m_d = links.send(buf(jd), buf(jd), mate)
        yield
        other = 1 - 2 * core
        links.arrived(buf(j + other), mate, own_m)
        links.arrived(buf(jp + other), mate, m_p)
        links.arrived(buf(jn + other), mate, m_n)
        links.arrived(buf(jd + other), mate, m_d)

    def chain(p):
        product(p, (x + 2) % NX, t.at[p, 0])
        got_p = links.send(t.at[p, 0, pl.ds(0, 2)], rxd.at[p, 0], xn)
        got_n = links.send(t.at[p, 0, pl.ds(2, 2)], rxd.at[p, 1], xp)
        yield
        product(p, (x + 1) % NX, t.at[p, 1])
        pure_p = links.send(t.at[p, 1, pl.ds(2, 2)], rx.at[p, 0, pl.ds(2, 2)], xn)
        yield
        product(p, (x + 3) % NX, t.at[p, 2])
        pure_n = links.send(t.at[p, 2, pl.ds(0, 2)], rx.at[p, 1, pl.ds(0, 2)], xp)
        yield
        links.arrived(rxd.at[p, 0], xp, got_p)
        t[p, 1, 0:2] = (t[p, 1, 0:2].astype(F32) + rxd[p, 0].astype(F32)).astype(BF16)
        sum_p = links.send(t.at[p, 1, pl.ds(0, 2)], rx.at[p, 0, pl.ds(0, 2)], xn)
        links.arrived(rxd.at[p, 1], xn, got_n)
        t[p, 2, 2:4] = (t[p, 2, 2:4].astype(F32) + rxd[p, 1].astype(F32)).astype(BF16)
        sum_n = links.send(t.at[p, 2, pl.ds(2, 2)], rx.at[p, 1, pl.ds(2, 2)], xp)
        yield
        product(p, x, town.at[p])
        yield
        links.arrived(rx.at[p, 0, pl.ds(2, 2)], xp, pure_p)
        links.arrived(rx.at[p, 1, pl.ds(0, 2)], xn, pure_n)
        links.arrived(rx.at[p, 0, pl.ds(0, 2)], xp, sum_p)
        links.arrived(rx.at[p, 1, pl.ds(2, 2)], xn, sum_n)

        def total(k):
            return town[p, k] + rx[p, 0, k].astype(F32) + rx[p, 1, k].astype(F32)

        s1[p, 0] = total(zh_d).astype(BF16)
        got_p = links.send(s1.at[p, 0, lo], rzd.at[p, 0], zhn)
        got_n = links.send(s1.at[p, 0, hi], rzd.at[p, 1], zhp)
        s1[p, 1] = total(zh_n).astype(BF16)
        pure_p = links.send(s1.at[p, 1, hi], rz.at[p, 0, hi], zhn)
        s1[p, 2] = total(zh_p).astype(BF16)
        pure_n = links.send(s1.at[p, 2, lo], rz.at[p, 1, lo], zhp)
        s1own[p] = total(zh)
        yield
        links.arrived(rzd.at[p, 0], zhp, got_p)
        s1[p, 1, lo] = (s1[p, 1, lo].astype(F32) + rzd[p, 0].astype(F32)).astype(BF16)
        sum_p = links.send(s1.at[p, 1, lo], rz.at[p, 0, lo], zhn)
        links.arrived(rzd.at[p, 1], zhn, got_n)
        s1[p, 2, hi] = (s1[p, 2, hi].astype(F32) + rzd[p, 1].astype(F32)).astype(BF16)
        sum_n = links.send(s1.at[p, 2, hi], rz.at[p, 1, hi], zhp)
        yield
        links.arrived(rz.at[p, 0, hi], zhp, pure_p)
        links.arrived(rz.at[p, 1, lo], zhn, pure_n)
        links.arrived(rz.at[p, 0, lo], zhp, sum_p)
        links.arrived(rz.at[p, 1, hi], zhn, sum_n)
        total_sum = s1own[p] + rz[p, 0].astype(F32) + rz[p, 1].astype(F32)
        if p == 0:
            column = (-total_sum).astype(BF16)
            c1_ref[...] = column
        else:
            column = (-(total_sum + nn_dot(c1_ref[...], inner[...]))).astype(BF16)
            c2_ref[...] = column
        g[p, j] = column
        yield from over_x_core(
            lambda k: g.at[p, k], lambda k, h: g.at[p, k, pl.ds(half * h, half)]
        )

        if p == 0:
            links.arrived(mx, mate, own_slot, own_self)
        sides = (0, 1) if p == 0 else (1,)
        n = 64 * len(sides)
        xg, part, recv, back = ((xg0, part0, recv0, back0), (xg1, part1, recv1, back1))[p]
        for k, m in enumerate(sides):
            found = nn_dot(mx[m], g[p].reshape(BLOCK, W))
            for d in range(NY):
                rows = found[:, 128 * d : 128 * d + 128]
                step = n // 8
                part[d, pl.ds(64 // step * k, 64 // step)] = rows.reshape(
                    64 // step, step, 128
                ).astype(part.dtype)
        out_slot, back_slot = links.slot(), links.slot()

        def to_all(copy_of):
            def start(e, _):
                copy_of(e).start()
                return 0

            lax.fori_loop(1, 32, start, 0)

        def piece(e):
            peer_y, peer_z = yz_peer(e)
            return links.make(
                part.at[peer_y, peer_z], recv.at[e - 1], at(yy=peer_y, zz=peer_z), out_slot
            )

        to_all(piece)
        every = links.make(recv, recv, mate, out_slot)
        links.pending.append((every, None))
        yield
        every.wait_recv()
        total_yz = part[y, z].astype(F32)
        for e in range(1, 32):
            total_yz = total_yz + recv[e - 1].astype(F32)
        back[y, z] = total_yz.astype(back.dtype)

        def reply(e):
            peer_y, peer_z = yz_peer(e)
            return links.make(
                back.at[y, z], back.at[y, z], at(yy=peer_y, zz=peer_z), back_slot
            )

        to_all(reply)
        every = links.make(recv, recv, mate, back_slot)
        links.pending.append((every, None))
        yield
        every.wait_recv()
        xg[j] = back[...].reshape(NY, n, 128).astype(BF16)
        yield from over_x_core(lambda k: xg.at[k], lambda k, h: xg.at[k, pl.ds(2 * h, 2)])
        yield

    parts = {
        "f": panel_gather(0),
        "s": panel_gather(1),
        "A": chain(0),
        "B": chain(1),
    }
    for name in ORDER:
        if name == "m":
            links.arrived(ax, mate, a_slot)
            mask_rows(ax, c + 1 - 2 * core)
        elif name == "o":
            send_own_rows()
        elif name == "t":
            spread_panel(1)
        else:
            next(parts[name])
    links.drain()


ORDER = "mftffsofsffAsAAsAsAsBBBABABAABAABBBABBABABABABB"
N_COPIES = 128


def finish(
        inner_ref,
    pivot1_ref,
    pivot2_ref,
    xg0,
    xg1,
    c1_ref,
    c2_ref,
    d1_out,
    i2_out,
    d2_out,
    c1_out,
    c2_out,
    d1,
    i2,
    d2,
    crossed,
    sem,
):
    def assemble(out, source, first, pivot):
        for k in range(8):
            for d in range(NY):
                for i in range(4):
                    start = 16 * (8 * i + k)
                    rows, cols = slice(start, start + 16), slice(128 * d, 128 * d + 128)
                    part = source[k, d, first + 16 * i : first + 16 * i + 16].astype(F32)
                    out[rows, cols] = part if pivot is None else pivot[rows, cols] - part

    def parts_dot(dot, wide):
        high = wide.astype(BF16)
        low = (wide - high.astype(F32)).astype(BF16)
        return dot(high) + dot(low)

    copies = [
        pltpu.make_async_copy(c1_ref, c1_out, sem.at[3]),
        pltpu.make_async_copy(c2_ref, c2_out, sem.at[4]),
        pltpu.make_async_copy(d1, d1_out, sem.at[0]),
        pltpu.make_async_copy(i2, i2_out, sem.at[1]),
        pltpu.make_async_copy(d2, d2_out, sem.at[2]),
    ]
    copies[0].start()
    copies[1].start()
    inner = inner_ref[...]
    assemble(d1, xg0, 0, pivot1_ref)
    copies[2].start()
    assemble(crossed, xg0, 64, None)
    i2[...] = -(parts_dot(lambda v: nn_dot(v, inner), d1[...]) + crossed[...].T)
    copies[3].start()
    inner_t = inner.T
    assemble(d2, xg1, 0, pivot2_ref)
    d2[...] = d2[...] - parts_dot(lambda v: nn_dot(inner_t, v), i2[...])
    copies[4].start()
    for copy in copies:
        copy.wait()


def body(
    ancestor_inverse,
    tile_pattern,
    rows_first,
    rows_second,
    panel_first,
    panel_second,
    inner_panel,
    pivot_first,
    pivot_second,
):
    col_block = ancestor_inverse.shape[1]
    halves = ancestor_inverse.reshape(NZH, NX, NC, SHARE, col_block)
    anywhere = pl.BlockSpec(memory_space=pl.ANY)
    in_hbm = pl.BlockSpec(memory_space=pltpu.HBM)
    vmem = pl.BlockSpec(memory_space=pltpu.VMEM)
    wide = jax.ShapeDtypeStruct((W, W), F32)
    column_first, column_second, gathered0, gathered1 = pl.pallas_call(
        kernel,
        out_shape=(
            jax.ShapeDtypeStruct((SHARE, W), BF16),
            jax.ShapeDtypeStruct((SHARE, W), BF16),
            jax.ShapeDtypeStruct((8, NY, 128, 128), BF16),
            jax.ShapeDtypeStruct((8, NY, 64, 128), BF16),
        ),
        in_specs=[in_hbm] * 7,
        out_specs=(vmem, vmem, vmem, vmem),
        scratch_shapes=[
            pltpu.VMEM((NZH, NX, SHARE, BLOCK), BF16),
            pltpu.VMEM((NZH, NX, SHARE, BLOCK), BF16),
            pltpu.SMEM((64, 64), jnp.int32),
            pltpu.VMEM((2, 16, 3072), BF16),
            pltpu.VMEM((2, 24, 128), jnp.int32),
            pltpu.VMEM((W, W), BF16),
            pltpu.VMEM((2, 16, 3072), BF16),
            pltpu.VMEM((8, 2, 64, BLOCK), BF16),
            pltpu.VMEM((8, 2, 64, BLOCK), BF16),
            pltpu.VMEM((2, 64, BLOCK), BF16),
            pltpu.VMEM((2, 3, NZH, SHARE, W), BF16),
            pltpu.VMEM((2, NZH, SHARE, W), F32),
            pltpu.VMEM((2, 2, 2, SHARE, W), BF16),
            pltpu.VMEM((2, 2, NZH, SHARE, W), BF16),
            pltpu.VMEM((2, 3, SHARE, W), BF16),
            pltpu.VMEM((2, SHARE, W), F32),
            pltpu.VMEM((2, 2, SHARE // 2, W), BF16),
            pltpu.VMEM((2, 2, SHARE, W), BF16),
            pltpu.VMEM((2, 8, SHARE, W), BF16),
            pltpu.VMEM((NY, 8, 16, 128), BF16),
            pltpu.VMEM((31, 16, 128), BF16),
            pltpu.VMEM((NY, 8, 16, 128), BF16),
            pltpu.VMEM((NY, 8, 8, 128), F32),
            pltpu.VMEM((31, 8, 128), F32),
            pltpu.VMEM((NY, 8, 8, 128), F32),
            pltpu.SemaphoreType.DMA((N_COPIES,)),
            pltpu.SemaphoreType.DMA((N_COPIES,)),
            pltpu.SemaphoreType.DMA((9,)),
        ],
        compiler_params=pltpu.CompilerParams(
            collective_id=0, has_side_effects=True, vmem_limit_bytes=48 * 2**20
        ),
    )(
        *(
            pltpu.with_memory_space_constraint(array, pltpu.HBM)
            for array in (
                halves,
                tile_pattern,
                panel_first.T,
                panel_second.T,
                rows_first.reshape(-1, 128),
                rows_second.reshape(-1, 128),
                inner_panel,
            )
        )
    )
    narrow = jax.ShapeDtypeStruct((SHARE, W), BF16)
    diagonal_first, inner_second, diagonal_second, column_first, column_second = pl.pallas_call(
        finish,
        out_shape=(wide, wide, wide, narrow, narrow),
        in_specs=[vmem] * 7,
        out_specs=(anywhere,) * 5,
        scratch_shapes=[pltpu.VMEM((W, W), F32)] * 4 + [pltpu.SemaphoreType.DMA((5,))],
        compiler_params=pltpu.CompilerParams(vmem_limit_bytes=32 * 2**20),
    )(
        inner_panel, pivot_first, pivot_second, gathered0, gathered1, column_first, column_second
    )
    return (column_first, diagonal_first, inner_second, column_second, diagonal_second)


def solution(mesh):
    return jax.shard_map(
        body,
        mesh=mesh,
        in_specs=(
            P("prow", "pcol"),
            P(),
            P(),
            P(),
            P("prow", "pcol"),
            P("prow", "pcol"),
            P(),
            P(),
            P(),
        ),
        out_specs=(P(("prow", "pcol"), None), P(), P(), P(("prow", "pcol"), None), P()),
        check_vma=False,
    )
```

```python
import jax
import jax.numpy as jnp
from jax import lax
from jax.experimental import pallas as pl
from jax.experimental.pallas import tpu as pltpu
from jax.sharding import PartitionSpec as P

TILE = 384
MESH = pl.DeviceIdType.MESH
BF16 = jnp.bfloat16
F32 = jnp.float32

NY, NX, NZH, NZL, NC = 4, 4, 4, 2, 2
BLOCK = 768
SHARE = 96
W = 512


def nt_dot(left, right):
    return lax.dot_general(left, right, (((1,), (1,)), ((), ())), preferred_element_type=F32)


def nn_dot(left, right):
    return jnp.dot(left, right, preferred_element_type=F32)


class Links:
    def __init__(self, send_sem, recv_sem):
        self.send_sem = send_sem
        self.recv_sem = recv_sem
        self.used = 0
        self.pending = []

    def slot(self):
        self.used += 1
        return self.used - 1

    def make(self, src, dst, device, slot):
        return pltpu.make_async_remote_copy(
            src_ref=src,
            dst_ref=dst,
            send_sem=self.send_sem.at[slot],
            recv_sem=self.recv_sem.at[slot],
            device_id=device,
            device_id_type=MESH,
        )

    def send(self, src, dst, device, slot=None, unless=None):
        slot = self.slot() if slot is None else slot
        copy = self.make(src, dst, device, slot)
        if unless is None:
            copy.start()
        else:
            pl.when(jnp.logical_not(unless))(copy.start)
        self.pending.append((copy, unless))
        return slot

    def arrived(self, ref, device, slot, unless=None):
        copy = self.make(ref, ref, device, slot)
        if unless is None:
            copy.wait_recv()
        else:
            pl.when(jnp.logical_not(unless))(copy.wait_recv)

    def drain(self):
        for copy, unless in self.pending:
            if unless is None:
                copy.wait_send()
            else:
                pl.when(jnp.logical_not(unless))(copy.wait_send)
        self.pending = []


def kernel(
    a_ref,
    pattern_ref,
    panel1_ref,
    panel2_ref,
    rows1_ref,
    rows2_ref,
    inner_ref,
    c1_ref,
    c2_ref,
    xg0,
    xg1,
    ao,
    ax,
    pattern,
    panels,
    rows,
    inner,
    xt,
    pt,
    ptx,
    mx,
    t,
    town,
    rxd,
    rx,
    s1,
    s1own,
    rzd,
    rz,
    g,
    part0,
    recv0,
    back0,
    part1,
    recv1,
    back1,
    send_sem,
    recv_sem,
    local_sem,
):
    r = lax.axis_index("prow")
    c = lax.axis_index("pcol")
    y = r % NY
    zl = r // NY
    zh = c // 8
    x = (c // 2) % NX
    core = c % 2
    j = c % 8
    z = zh * 2 + zl

    def at(yy=None, zz=None, xx=None, cc=None):
        yy = y if yy is None else yy
        zz = z if zz is None else zz
        xx = x if xx is None else xx
        cc = core if cc is None else cc
        return ((zz % 2) * NY + yy, (zz // 2) * 8 + xx * 2 + cc)

    mate = at(cc=1 - core)
    xn, xp = at(xx=(x + 1) % NX), at(xx=(x + 3) % NX)
    zhn, zhp = at(zz=(z + 2) % 8), at(zz=(z + 6) % 8)
    yn, yp = at(yy=(y + 1) % NY), at(yy=(y + 3) % NY)
    zmate = at(zz=zh * 2 + 1 - zl)
    def yz_peer(e):
        return (y + e // 8) % NY, (z + e % 8) % 8

    barrier = pltpu.get_barrier_semaphore()
    held = zl * NY + (y + 8 - c // 4) % NY
    first_self = (c // 4 == r) & (held == r)
    own_self = (c // 4 == r) & (8 * (c % 4) + held == c)
    for device in [mate, xn, xp]:
        pl.semaphore_signal(barrier, inc=1, device_id=device, device_id_type=MESH)

    def greet(e, _):
        peer_y, peer_z = yz_peer(e)
        pl.semaphore_signal(
            barrier, inc=1, device_id=at(yy=peer_y, zz=peer_z), device_id_type=MESH
        )
        return 0

    lax.fori_loop(1, 32, greet, 0)
    for i in range(4):

        @pl.when(jnp.logical_not(first_self & (c % 4 == i)))
        def _():
            pl.semaphore_signal(barrier, inc=1, device_id=(c // 4, 4 * held + i), device_id_type=MESH)

    @pl.when(jnp.logical_not(own_self))
    def _():
        pl.semaphore_signal(barrier, inc=1, device_id=(j // 4 * NY + (j + r) % NY, 4 * r + zh), device_id_type=MESH)

    own_rows = pl.ds(pl.multiple_of(24 * r, 8), 24)
    loads = [
        pltpu.make_async_copy(rows1_ref.at[own_rows], rows.at[0], local_sem.at[3]),
        pltpu.make_async_copy(rows2_ref.at[own_rows], rows.at[1], local_sem.at[4]),
        pltpu.make_async_copy(panel1_ref, panels.at[0], local_sem.at[5]),
        pltpu.make_async_copy(panel2_ref, panels.at[1], local_sem.at[6]),
        pltpu.make_async_copy(pattern_ref, pattern, local_sem.at[7]),
        pltpu.make_async_copy(a_ref.at[:, :, core], ao, local_sem.at[0]),
        pltpu.make_async_copy(inner_ref, inner, local_sem.at[8]),
    ]
    for load in loads:
        load.start()
    for load in loads[:4]:
        load.wait()
    keep1 = rows[0].astype(F32)
    keep2 = keep1 * rows[1].astype(F32)
    for p, keep in enumerate((keep1, keep2)):
        for k in range(24):
            cut = slice(128 * k, 128 * k + 128)
            xt[p, :, cut] = (panels[p, :, cut].astype(F32) * keep[k : k + 1]).astype(BF16)

    pl.semaphore_wait(
        barrier, 34 + 5 - first_self.astype(jnp.int32) - own_self.astype(jnp.int32)
    )

    links = Links(send_sem, recv_sem)

    slice16 = pl.ds(pl.multiple_of(16 * (c % 4), 16), 16)
    base_first = [links.slot() for _ in range(8)][0]
    own_slot = links.slot()

    def spread(source, target, base, device, me, q, spare):
        copy = pltpu.make_async_remote_copy(
            src_ref=source,
            dst_ref=target,
            send_sem=send_sem.at[base + q],
            recv_sem=recv_sem.at[base + c % 4],
            device_id=device,
            device_id_type=MESH,
        )
        pl.when(jnp.logical_not(me))(copy.start)
        links.pending.append((copy, me))

        @pl.when(me)
        def _():
            local = pltpu.make_async_copy(source, target, local_sem.at[spare])
            local.start()
            local.wait()

    def spread_panel(p):
        for q in range(4):
            spread(
                xt.at[p, :, pl.ds(768 * q, 768)],
                pt.at[c // 4, p, slice16, :],
                base_first + 4 * p,
                (c // 16 * NY + (c // 4 + r) % NY, 4 * r + q),
                first_self & (c % 4 == q),
                q,
                1,
            )

    spread_panel(0)

    a_slot = links.send(a_ref.at[:, :, 1 - core], ax, mate)

    def send_own_rows():
        links.send(pt.at[held], mx, (c // 4, 8 * (c % 4) + held), own_slot, own_self)

        @pl.when(own_self)
        def _():
            local = pltpu.make_async_copy(pt.at[held], mx, local_sem.at[2])
            local.start()
            local.wait()

    def mask_rows(ref, owner):
        def chunk(i, _):
            m = i // NX
            n = i % NX
            for k in range(2):
                cut = slice(TILE * k, TILE * k + TILE)
                keep = pattern[8 * r + 2 * m + n // 2, 2 * owner + k].astype(F32)
                ref[m, n, :, cut] = (ref[m, n, :, cut].astype(F32) * keep).astype(BF16)
            return 0

        lax.fori_loop(0, NZH * NX, chunk, 0)

    for load in loads[4:]:
        load.wait()
    mask_rows(ao, c)

    def row_of(yy, zz):
        return zz * NY + (yy + 8 - c // 4) % NY

    r_z = row_of(y, 1 - zl)
    y_p, y_n, y_d = (y + 3) % NY, (y + 1) % NY, (y + 2) % NY

    def panel_gather(p):
        forwarded = []

        def to(device, row):
            return links.send(pt.at[row, p], pt.at[row, p], device)

        def to_mate(row):
            forwarded.append((row, links.send(pt.at[row, p], ptx.at[row, p], mate)))

        def part(row, h):
            return pt.at[row, p, pl.ds(32 * h, 32)]

        for i in range(4):
            links.arrived(
                pt.at[held, p, pl.ds(16 * i, 16), :],
                mate,
                base_first + 4 * p + i,
                first_self & (c % 4 == i),
            )
        got_z, got_yp, got_yn = to(zmate, held), to(yn, held), to(yp, held)
        to_mate(held)
        yield
        links.arrived(pt.at[r_z, p], zmate, got_z)
        got_yp_z, got_yn_z = to(yn, r_z), to(yp, r_z)
        to_mate(r_z)
        yield
        relayed = []
        for zz, slot_p, slot_n in ((zl, got_yp, got_yn), (1 - zl, got_yp_z, got_yn_z)):
            row_p, row_n, row_d = row_of(y_p, zz), row_of(y_n, zz), row_of(y_d, zz)
            links.arrived(pt.at[row_p, p], yp, slot_p)
            got_d0 = links.send(part(row_p, 0), part(row_p, 0), yn)
            links.arrived(pt.at[row_n, p], yn, slot_n)
            got_d1 = links.send(part(row_n, 1), part(row_n, 1), yp)
            to_mate(row_p)
            to_mate(row_n)
            relayed.append((row_d, got_d0, got_d1))
            yield
        for row_d, got_d0, got_d1 in relayed:
            links.arrived(part(row_d, 0), yp, got_d0)
            links.arrived(part(row_d, 1), yn, got_d1)
            to_mate(row_d)
        yield
        for row, slot in forwarded:
            links.arrived(ptx.at[row, p], mate, slot)
        yield

    def product(p, xx, out):
        left = ao[:, xx].reshape(NZH * SHARE, BLOCK)
        left_x = ax[:, xx].reshape(NZH * SHARE, BLOCK)
        for h in range(2):
            right = pt[pl.ds(4 * h, 4), p].reshape(256, BLOCK)
            right_x = ptx[pl.ds(4 * h, 4), p].reshape(256, BLOCK)
            value = nt_dot(left, right) + nt_dot(left_x, right_x)
            out[..., pl.ds(256 * h, 256)] = value.reshape(NZH, SHARE, 256).astype(out.dtype)

    half = SHARE // 2
    lo, hi = pl.ds(0, half), pl.ds(half, half)
    zh_n, zh_p, zh_d = (zh + 1) % NZH, (zh + 3) % NZH, (zh + 2) % NZH
    jn, jp, jd = (j + 2) % 8, (j + 6) % 8, (j + 4) % 8

    def over_x_core(buf, part):
        own_p = links.send(buf(j), buf(j), xn)
        own_n = links.send(buf(j), buf(j), xp)
        own_m = links.send(buf(j), buf(j), mate)
        yield
        links.arrived(buf(jp), xp, own_p)
        d0 = links.send(part(jp, 0), part(jp, 0), xn)
        links.arrived(buf(jn), xn, own_n)
        d1 = links.send(part(jn, 1), part(jn, 1), xp)
        m_p = links.send(buf(jp), buf(jp), mate)
        m_n = links.send(buf(jn), buf(jn), mate)
        yield
        links.arrived(part(jd, 0), xp, d0)
        links.arrived(part(jd, 1), xn, d1)
        m_d = links.send(buf(jd), buf(jd), mate)
        yield
        other = 1 - 2 * core
        links.arrived(buf(j + other), mate, own_m)
        links.arrived(buf(jp + other), mate, m_p)
        links.arrived(buf(jn + other), mate, m_n)
        links.arrived(buf(jd + other), mate, m_d)

    def chain(p):
        product(p, (x + 2) % NX, t.at[p, 0])
        got_p = links.send(t.at[p, 0, pl.ds(0, 2)], rxd.at[p, 0], xn)
        got_n = links.send(t.at[p, 0, pl.ds(2, 2)], rxd.at[p, 1], xp)
        yield
        product(p, (x + 1) % NX, t.at[p, 1])
        pure_p = links.send(t.at[p, 1, pl.ds(2, 2)], rx.at[p, 0, pl.ds(2, 2)], xn)
        yield
        product(p, (x + 3) % NX, t.at[p, 2])
        pure_n = links.send(t.at[p, 2, pl.ds(0, 2)], rx.at[p, 1, pl.ds(0, 2)], xp)
        yield
        links.arrived(rxd.at[p, 0], xp, got_p)
        t[p, 1, 0:2] = (t[p, 1, 0:2].astype(F32) + rxd[p, 0].astype(F32)).astype(BF16)
        sum_p = links.send(t.at[p, 1, pl.ds(0, 2)], rx.at[p, 0, pl.ds(0, 2)], xn)
        links.arrived(rxd.at[p, 1], xn, got_n)
        t[p, 2, 2:4] = (t[p, 2, 2:4].astype(F32) + rxd[p, 1].astype(F32)).astype(BF16)
        sum_n = links.send(t.at[p, 2, pl.ds(2, 2)], rx.at[p, 1, pl.ds(2, 2)], xp)
        yield
        product(p, x, town.at[p])
        yield
        links.arrived(rx.at[p, 0, pl.ds(2, 2)], xp, pure_p)
        links.arrived(rx.at[p, 1, pl.ds(0, 2)], xn, pure_n)
        links.arrived(rx.at[p, 0, pl.ds(0, 2)], xp, sum_p)
        links.arrived(rx.at[p, 1, pl.ds(2, 2)], xn, sum_n)

        def total(k):
            return town[p, k] + rx[p, 0, k].astype(F32) + rx[p, 1, k].astype(F32)

        s1[p, 0] = total(zh_d).astype(BF16)
        got_p = links.send(s1.at[p, 0, lo], rzd.at[p, 0], zhn)
        got_n = links.send(s1.at[p, 0, hi], rzd.at[p, 1], zhp)
        s1[p, 1] = total(zh_n).astype(BF16)
        pure_p = links.send(s1.at[p, 1, hi], rz.at[p, 0, hi], zhn)
        s1[p, 2] = total(zh_p).astype(BF16)
        pure_n = links.send(s1.at[p, 2, lo], rz.at[p, 1, lo], zhp)
        s1own[p] = total(zh)
        yield
        links.arrived(rzd.at[p, 0], zhp, got_p)
        s1[p, 1, lo] = (s1[p, 1, lo].astype(F32) + rzd[p, 0].astype(F32)).astype(BF16)
        sum_p = links.send(s1.at[p, 1, lo], rz.at[p, 0, lo], zhn)
        links.arrived(rzd.at[p, 1], zhn, got_n)
        s1[p, 2, hi] = (s1[p, 2, hi].astype(F32) + rzd[p, 1].astype(F32)).astype(BF16)
        sum_n = links.send(s1.at[p, 2, hi], rz.at[p, 1, hi], zhp)
        yield
        links.arrived(rz.at[p, 0, hi], zhp, pure_p)
        links.arrived(rz.at[p, 1, lo], zhn, pure_n)
        links.arrived(rz.at[p, 0, lo], zhp, sum_p)
        links.arrived(rz.at[p, 1, hi], zhn, sum_n)
        total_sum = s1own[p] + rz[p, 0].astype(F32) + rz[p, 1].astype(F32)
        if p == 0:
            column = (-total_sum).astype(BF16)
            c1_ref[...] = column
        else:
            column = (-(total_sum + nn_dot(c1_ref[...], inner[...]))).astype(BF16)
            c2_ref[...] = column
        g[p, j] = column
        yield from over_x_core(
            lambda k: g.at[p, k], lambda k, h: g.at[p, k, pl.ds(half * h, half)]
        )

        if p == 0:
            links.arrived(mx, mate, own_slot, own_self)
        sides = (0, 1) if p == 0 else (1,)
        n = 64 * len(sides)
        xg, part, recv, back = ((xg0, part0, recv0, back0), (xg1, part1, recv1, back1))[p]
        for k, m in enumerate(sides):
            found = nn_dot(mx[m], g[p].reshape(BLOCK, W))
            for d in range(NY):
                rows = found[:, 128 * d : 128 * d + 128]
                step = n // 8
                part[d, pl.ds(64 // step * k, 64 // step)] = rows.reshape(
                    64 // step, step, 128
                ).astype(part.dtype)
        out_slot, back_slot = links.slot(), links.slot()

        def to_all(copy_of):
            def start(e, _):
                copy_of(e).start()
                return 0

            lax.fori_loop(1, 32, start, 0)

        def piece(e):
            peer_y, peer_z = yz_peer(e)
            return links.make(
                part.at[peer_y, peer_z], recv.at[e - 1], at(yy=peer_y, zz=peer_z), out_slot
            )

        to_all(piece)
        every = links.make(recv, recv, mate, out_slot)
        links.pending.append((every, None))
        yield
        every.wait_recv()
        total_yz = part[y, z].astype(F32)
        for e in range(1, 32):
            total_yz = total_yz + recv[e - 1].astype(F32)
        back[y, z] = total_yz.astype(back.dtype)

        def reply(e):
            peer_y, peer_z = yz_peer(e)
            return links.make(
                back.at[y, z], back.at[y, z], at(yy=peer_y, zz=peer_z), back_slot
            )

        to_all(reply)
        every = links.make(recv, recv, mate, back_slot)
        links.pending.append((every, None))
        yield
        every.wait_recv()
        xg[j] = back[...].reshape(NY, n, 128).astype(BF16)
        yield from over_x_core(lambda k: xg.at[k], lambda k, h: xg.at[k, pl.ds(2 * h, 2)])
        yield

    parts = {
        "f": panel_gather(0),
        "s": panel_gather(1),
        "A": chain(0),
        "B": chain(1),
    }
    for name in ORDER:
        if name == "m":
            links.arrived(ax, mate, a_slot)
            mask_rows(ax, c + 1 - 2 * core)
        elif name == "o":
            send_own_rows()
        elif name == "t":
            spread_panel(1)
        else:
            next(parts[name])
    links.drain()


ORDER = "mftffsofsffAsAAsAsAsBBBABABAABAABBBABBABABABABB"
N_COPIES = 128


def finish(
        inner_ref,
    pivot1_ref,
    pivot2_ref,
    xg0,
    xg1,
    c1_ref,
    c2_ref,
    d1_out,
    i2_out,
    d2_out,
    c1_out,
    c2_out,
    d1,
    i2,
    d2,
    crossed,
    sem,
):
    def assemble(out, source, first, pivot):
        for k in range(8):
            for d in range(NY):
                rows, cols = slice(64 * k, 64 * k + 64), slice(128 * d, 128 * d + 128)
                part = source[k, d, first : first + 64].astype(F32)
                out[rows, cols] = part if pivot is None else pivot[rows, cols] - part

    def parts_dot(dot, wide):
        high = wide.astype(BF16)
        low = (wide - high.astype(F32)).astype(BF16)
        return dot(high) + dot(low)

    copies = [
        pltpu.make_async_copy(c1_ref, c1_out, sem.at[3]),
        pltpu.make_async_copy(c2_ref, c2_out, sem.at[4]),
        pltpu.make_async_copy(d1, d1_out, sem.at[0]),
        pltpu.make_async_copy(i2, i2_out, sem.at[1]),
        pltpu.make_async_copy(d2, d2_out, sem.at[2]),
    ]
    copies[0].start()
    copies[1].start()
    inner = inner_ref[...]
    assemble(d1, xg0, 0, pivot1_ref)
    copies[2].start()
    assemble(crossed, xg0, 64, None)
    i2[...] = -(parts_dot(lambda v: nn_dot(v, inner), d1[...]) + crossed[...].T)
    copies[3].start()
    inner_t = inner.T
    assemble(d2, xg1, 0, pivot2_ref)
    d2[...] = d2[...] - parts_dot(lambda v: nn_dot(inner_t, v), i2[...])
    copies[4].start()
    for copy in copies:
        copy.wait()


def body(
    ancestor_inverse,
    tile_pattern,
    rows_first,
    rows_second,
    panel_first,
    panel_second,
    inner_panel,
    pivot_first,
    pivot_second,
):
    col_block = ancestor_inverse.shape[1]
    halves = ancestor_inverse.reshape(NZH, NX, NC, SHARE, col_block)
    anywhere = pl.BlockSpec(memory_space=pl.ANY)
    in_hbm = pl.BlockSpec(memory_space=pltpu.HBM)
    vmem = pl.BlockSpec(memory_space=pltpu.VMEM)
    wide = jax.ShapeDtypeStruct((W, W), F32)
    column_first, column_second, gathered0, gathered1 = pl.pallas_call(
        kernel,
        out_shape=(
            jax.ShapeDtypeStruct((SHARE, W), BF16),
            jax.ShapeDtypeStruct((SHARE, W), BF16),
            jax.ShapeDtypeStruct((8, NY, 128, 128), BF16),
            jax.ShapeDtypeStruct((8, NY, 64, 128), BF16),
        ),
        in_specs=[in_hbm] * 7,
        out_specs=(vmem, vmem, vmem, vmem),
        scratch_shapes=[
            pltpu.VMEM((NZH, NX, SHARE, BLOCK), BF16),
            pltpu.VMEM((NZH, NX, SHARE, BLOCK), BF16),
            pltpu.SMEM((64, 64), jnp.int32),
            pltpu.VMEM((2, 16, 3072), BF16),
            pltpu.VMEM((2, 24, 128), jnp.int32),
            pltpu.VMEM((W, W), BF16),
            pltpu.VMEM((2, 16, 3072), BF16),
            pltpu.VMEM((8, 2, 64, BLOCK), BF16),
            pltpu.VMEM((8, 2, 64, BLOCK), BF16),
            pltpu.VMEM((2, 64, BLOCK), BF16),
            pltpu.VMEM((2, 3, NZH, SHARE, W), BF16),
            pltpu.VMEM((2, NZH, SHARE, W), F32),
            pltpu.VMEM((2, 2, 2, SHARE, W), BF16),
            pltpu.VMEM((2, 2, NZH, SHARE, W), BF16),
            pltpu.VMEM((2, 3, SHARE, W), BF16),
            pltpu.VMEM((2, SHARE, W), F32),
            pltpu.VMEM((2, 2, SHARE // 2, W), BF16),
            pltpu.VMEM((2, 2, SHARE, W), BF16),
            pltpu.VMEM((2, 8, SHARE, W), BF16),
            pltpu.VMEM((NY, 8, 16, 128), BF16),
            pltpu.VMEM((31, 16, 128), BF16),
            pltpu.VMEM((NY, 8, 16, 128), BF16),
            pltpu.VMEM((NY, 8, 8, 128), F32),
            pltpu.VMEM((31, 8, 128), F32),
            pltpu.VMEM((NY, 8, 8, 128), F32),
            pltpu.SemaphoreType.DMA((N_COPIES,)),
            pltpu.SemaphoreType.DMA((N_COPIES,)),
            pltpu.SemaphoreType.DMA((9,)),
        ],
        compiler_params=pltpu.CompilerParams(
            collective_id=0, has_side_effects=True, vmem_limit_bytes=48 * 2**20
        ),
    )(
        *(
            pltpu.with_memory_space_constraint(array, pltpu.HBM)
            for array in (
                halves,
                tile_pattern,
                panel_first.T,
                panel_second.T,
                rows_first.reshape(-1, 128),
                rows_second.reshape(-1, 128),
                inner_panel,
            )
        )
    )
    narrow = jax.ShapeDtypeStruct((SHARE, W), BF16)
    diagonal_first, inner_second, diagonal_second, column_first, column_second = pl.pallas_call(
        finish,
        out_shape=(wide, wide, wide, narrow, narrow),
        in_specs=[vmem] * 7,
        out_specs=(anywhere,) * 5,
        scratch_shapes=[pltpu.VMEM((W, W), F32)] * 4 + [pltpu.SemaphoreType.DMA((5,))],
        compiler_params=pltpu.CompilerParams(vmem_limit_bytes=32 * 2**20),
    )(
        inner_panel, pivot_first, pivot_second, gathered0, gathered1, column_first, column_second
    )
    return (column_first, diagonal_first, inner_second, column_second, diagonal_second)


def solution(mesh):
    return jax.shard_map(
        body,
        mesh=mesh,
        in_specs=(
            P("prow", "pcol"),
            P(),
            P(),
            P(),
            P("prow", "pcol"),
            P("prow", "pcol"),
            P(),
            P(),
            P(),
        ),
        out_specs=(P(("prow", "pcol"), None), P(), P(), P(("prow", "pcol"), None), P()),
        check_vma=False,
    )
```
